32 devices in a mesh: ctx: 4 (over z), seq: 8 (over y, x, core).
Axes of the slice: x: 2, y: 2, z: 4, core: 2. Of those that a mesh axis runs over, the one named last changes fastest.
Arguments:
- queries: bfloat16 [8192, 128], P(('seq', 'ctx')), may hold values from -6 to 6
- keys: bfloat16 [8192, 128], P(('seq', 'ctx')), may hold values from -6 to 6
- values: bfloat16 [8192, 1024], P(('seq', 'ctx')), may hold values from -6 to 6
- grad_output: bfloat16 [8192, 1024], P(('seq', 'ctx')), may hold values from -6 to 6
Outputs:
- attended: bfloat16 [8192, 1024], P(('seq', 'ctx'))
- grad_queries: bfloat16 [8192, 128], P(('seq', 'ctx'))
- grad_keys: bfloat16 [8192, 128], P(('seq', 'ctx'))
- grad_values: bfloat16 [8192, 1024], P(('seq', 'ctx'))
The draws below stay inside these ranges and needn't reach their ends.
All inputs are finite; a program needn't handle non-finite values.
Results may differ from the reference program's by a relative error of at most 0.001.
Values sent between devices are 32-bit elements; how exact they have to be, the bound alone decides.
A program may use at most 128 MiB of HBM per device.

```python
import math
import jax
import jax.numpy as jnp
import numpy as np
from jax import lax

HEADS = 8
QK_DIM = 16
HEAD_DIM = 128
TOK_DEV = 256
FEATURES = 153
TOKENS = 8192


def levels(stream_key, dims, cuts, low, top_value):
    def one(dim, blocks):
        draws = jax.random.uniform(jax.random.fold_in(jax.random.fold_in(stream_key, 6), dim), (blocks,), jnp.float32, low / len(cuts), top_value / len(cuts))
        return jnp.repeat(jnp.exp(draws), dims[dim] // blocks).reshape((-1,) + (1,) * (len(dims) - dim - 1))

    level = one(*cuts[0])
    for cut in cuts[1:]:
        level = level * one(*cut)
    return level


def normal_values(stream_key, shape, scale, bound, cuts=(), kind=jnp.bfloat16):
    values = scale * jax.random.normal(stream_key, shape, jnp.float32)
    if cuts:
        values = values * levels(stream_key, shape, cuts, -0.22, 0.18)
    return jnp.clip(values, -bound, bound).astype(kind)


def setup_inputs(seed: int = 0) -> dict:
    streams_of = jax.random.split(jax.random.key(seed), 5)
    queries = normal_values(streams_of[0], (TOKENS, HEADS * QK_DIM), 1.0, 6.0, ((0, 32),))
    keys = normal_values(streams_of[1], (TOKENS, HEADS * QK_DIM), 1.0, 6.0, ((0, 32),))
    values = normal_values(streams_of[2], (TOKENS, HEADS * HEAD_DIM), 1.0, 6.0, ((0, 32),))
    grad_output = normal_values(streams_of[3], (TOKENS, HEADS * HEAD_DIM), 1.0, 6.0, ((0, 32),))
    return {"queries": queries, "keys": keys, "values": values, "grad_output": grad_output}


HIGHEST = lax.Precision.HIGHEST

def features(entries):
    width = entries.shape[1]
    upper, lower = np.triu_indices(width)
    factors = np.where(upper == lower, 1.0, math.sqrt(2.0)) / math.sqrt(2.0 * width)
    ones = jnp.ones_like(entries[:, :1, :])
    linear = entries / math.sqrt(math.sqrt(width))
    square = entries[:, upper, :] * entries[:, lower, :] * jnp.asarray(factors, entries.dtype)[None, :, None]
    return jnp.concatenate([ones, linear, square], axis=1)

def block_kernel(query, key_rows):
    length = query.shape[0]
    query_half = query.astype(jnp.bfloat16)
    key_half = key_rows.astype(jnp.bfloat16)
    dots = jnp.einsum('thd,shd->hts', query_half, key_half, preferred_element_type=jnp.float32) / math.sqrt(query.shape[-1])
    causal = jnp.arange(length)[:, None] >= jnp.arange(length)[None, :]
    kernel = jnp.where(causal[None], 1.0 + dots + 0.5 * dots * dots, 0.0)
    return (dots, kernel, causal)

def forward_block(left, kernel, value, prior_state, prior_norm):
    numer = jnp.einsum('hts,she->the', kernel, value, precision=HIGHEST)
    numer = numer + jnp.einsum('hft,hfe->the', left, prior_state, precision=HIGHEST)
    denom = lax.optimization_barrier(jnp.sum(kernel, axis=-1)).T + jnp.einsum('hft,hf->th', left, prior_norm, precision=HIGHEST)
    output = numer / denom[:, :, None]
    return (output, denom)

def later_terms(left, grad, output, denom):
    scaled = grad / denom[:, :, None]
    share = lax.optimization_barrier(jnp.sum(grad * output, axis=-1)) / denom
    term_state = jnp.einsum('hft,the->hfe', left, scaled, precision=HIGHEST)
    term_norm = jnp.einsum('hft,th->hf', left, share, precision=HIGHEST)
    return (scaled, share, term_state, term_norm)

def backward_block(query, key_rows, value, scaled, share, dots, kernel, causal, right, left_pull, right_pull, prior_state, prior_norm, later_state, later_norm):
    direct = jnp.einsum('the,she->hts', scaled, value, precision=HIGHEST) - share.T[:, :, None]
    grad_kernel = jnp.where(causal[None], direct, 0.0)
    grad_left = jnp.einsum('hfe,the->hft', prior_state, scaled, precision=HIGHEST) - prior_norm[:, :, None] * share.T[:, None, :]
    grad_right = jnp.einsum('hfe,she->hfs', later_state, value, precision=HIGHEST) - later_norm[:, :, None]
    grad_value = jnp.einsum('hts,the->she', kernel, scaled, precision=HIGHEST)
    grad_value = grad_value + jnp.einsum('hfs,hfe->she', right, later_state, precision=HIGHEST)
    grad_dots = grad_kernel * (1.0 + dots) / math.sqrt(query.shape[-1])
    grad_query = jnp.einsum('hts,shd->thd', grad_dots, key_rows, precision=HIGHEST)
    grad_query = grad_query + jnp.transpose(left_pull(grad_left)[0], (2, 0, 1))
    grad_key = jnp.einsum('hts,thd->shd', grad_dots, query, precision=HIGHEST)
    grad_key = grad_key + jnp.transpose(right_pull(grad_right)[0], (2, 0, 1))
    return (grad_query, grad_key, grad_value)

def reference(queries, keys, values, grad_output):
    blocks = TOKENS // TOK_DEV

    def split(array, width):
        return array.astype(jnp.float32).reshape(blocks, TOK_DEV, HEADS, width)
    query_blocks = split(queries, QK_DIM)
    key_blocks = split(keys, QK_DIM)
    value_blocks = split(values, HEAD_DIM)
    grad_blocks = split(grad_output, HEAD_DIM)

    def forward_step(carry, inputs):
        prior_state, prior_norm = carry
        query, key_rows, value, grad = inputs
        left = features(jnp.transpose(query, (1, 2, 0)))
        right = features(jnp.transpose(key_rows, (1, 2, 0)))
        dots, kernel, causal = block_kernel(query, key_rows)
        output, denom = forward_block(left, kernel, value, prior_state, prior_norm)
        scaled, share, term_state, term_norm = later_terms(left, grad, output, denom)
        state = jnp.einsum('hfs,she->hfe', right, value, precision=HIGHEST)
        norm = lax.optimization_barrier(jnp.sum(right, axis=-1))
        return ((prior_state + state, prior_norm + norm), (output, denom, prior_state, prior_norm, term_state, term_norm))
    start = (jnp.zeros((HEADS, FEATURES, HEAD_DIM), jnp.float32), jnp.zeros((HEADS, FEATURES), jnp.float32))
    final, stored = lax.scan(forward_step, start, (query_blocks, key_blocks, value_blocks, grad_blocks))
    outputs, denoms, prior_states, prior_norms, term_states, term_norms = stored

    def suffix_step(carry, inputs):
        return ((carry[0] + inputs[0], carry[1] + inputs[1]), carry)
    final_later, later = lax.scan(suffix_step, start, (term_states, term_norms), reverse=True)
    later_states, later_norms = later

    def backward_one(inputs):
        query, key_rows, value, grad, output, denom, prior_state, prior_norm, later_state, later_norm = inputs
        left, left_pull = jax.vjp(features, jnp.transpose(query, (1, 2, 0)))
        right, right_pull = jax.vjp(features, jnp.transpose(key_rows, (1, 2, 0)))
        dots, kernel, causal = block_kernel(query, key_rows)
        scaled, share, term_state, term_norm = later_terms(left, grad, output, denom)
        return backward_block(query, key_rows, value, scaled, share, dots, kernel, causal, right, left_pull, right_pull, prior_state, prior_norm, later_state, later_norm)
    grad_query, grad_key, grad_value = lax.map(backward_one, (query_blocks, key_blocks, value_blocks, grad_blocks, outputs, denoms, prior_states, prior_norms, later_states, later_norms))
    attended = outputs.reshape(TOKENS, HEADS * HEAD_DIM).astype(jnp.bfloat16)
    return (attended, grad_query.reshape(TOKENS, HEADS * QK_DIM).astype(jnp.bfloat16), grad_key.reshape(TOKENS, HEADS * QK_DIM).astype(jnp.bfloat16), grad_value.reshape(TOKENS, HEADS * HEAD_DIM).astype(jnp.bfloat16))
```

```python
import functools
import math

import jax
import jax.numpy as jnp
from jax import lax
from jax.experimental import pallas as pl
from jax.experimental.pallas import tpu as pltpu
from jax.sharding import PartitionSpec as P

HEADS = 8
QK_DIM = 16
HEAD_DIM = 128
LANES = 128
ROWS = 160
HALF = ROWS // 2
MESH = pl.DeviceIdType.MESH
NN = (((1,), (0,)), ((), ()))
NT = (((1,), (1,)), ((), ()))
TN = (((0,), (0,)), ((), ()))
F32 = jnp.float32
BF16 = jnp.bfloat16


def dot(a, b, dims=NN):
    return lax.dot_general(a, b, dims, preferred_element_type=F32)


def split(x):
    high = x.astype(BF16)
    return high, (x - high.astype(F32)).astype(BF16)


def dot2(pair, b, dims=NN):
    return dot(pair[0], b, dims) + dot(pair[1], b, dims)


def dot2r(a, pair, dims=NN):
    return dot(a, pair[0], dims) + dot(a, pair[1], dims)


def iota(shape, dim):
    return lax.broadcasted_iota(jnp.int32, shape, dim)


def shifted(x, d):
    return pltpu.roll(x, d % QK_DIM, 0)


def features(x):
    half = QK_DIM // 2
    parts = [x, x * x]
    for d in range(1, half):
        parts.append(x * shifted(x, -d))
    parts.append(x[:half] * x[half:])
    parts.append(jnp.where(iota((8, x.shape[1]), 0) == 0, 1.0, 0.0))
    return jnp.concatenate(parts, axis=0)


def weighed(state):
    w = QK_DIM
    last = ROWS - 8
    return jnp.concatenate(
        [
            state[:w] * (1.0 / math.sqrt(w)),
            state[w : 2 * w] * (0.5 / w),
            state[2 * w : last] * (1.0 / w),
            state[last:],
        ],
        axis=0,
    )


def pull(grad, x):
    w, half = QK_DIM, QK_DIM // 2
    total = grad[:w] + 2.0 * grad[w : 2 * w] * x
    for d in range(1, half):
        rows = grad[w * (d + 1) : w * (d + 2)]
        total = total + rows * shifted(x, -d) + shifted(rows * x, d)
    rows = grad[w * (half + 1) : w * (half + 1) + half]
    return total + jnp.concatenate([rows * x[half:], rows * x[:half]], axis=0)


def own_block():
    return iota((LANES, LANES), 0) // QK_DIM == iota((LANES, LANES), 1) // QK_DIM


def compact(square):
    kept = jnp.where(own_block(), square, 0.0)
    total = kept[:QK_DIM]
    for h in range(1, HEADS):
        total = total + kept[h * QK_DIM : (h + 1) * QK_DIM]
    return total


def blocks(rows):
    return jnp.where(own_block(), jnp.concatenate([rows] * HEADS, axis=0), 0.0)


class Small:
    def __init__(self, n_ctx, n_seq, reverse, refs):
        self.own, self.got, self.total, self.kept, self.far, self.send_sem, self.recv_sem = refs
        self.n_ctx, self.n_seq, self.reverse = n_ctx, n_seq, reverse
        self.ctx, self.seq = lax.axis_index("ctx"), lax.axis_index("seq")

    def copy(self, source, target, n, device):
        return pltpu.make_async_remote_copy(
            src_ref=source,
            dst_ref=target,
            send_sem=self.send_sem.at[n],
            recv_sem=self.recv_sem.at[n],
            device_id=device,
            device_id_type=MESH,
        )

    def near_copy(self, i):
        return self.copy(
            self.own, self.got.at[i - 1], i - 1, (lax.rem(self.ctx + i, self.n_ctx), self.seq)
        )

    def far_copy(self, i):
        return self.copy(
            self.total,
            self.far.at[i - 1],
            self.n_ctx - 2 + i,
            (self.ctx, lax.rem(self.seq + i, self.n_seq)),
        )

    def before(self, place, i):
        return place < i if self.reverse else place >= i

    def start(self):
        for i in range(1, self.n_ctx):
            self.near_copy(i).start()

    def turn(self):
        total = self.own[...]
        kept = jnp.zeros_like(total)
        for i in range(1, self.n_ctx):
            self.near_copy(i).wait_recv()
            arrived = self.got[i - 1]
            total = total + arrived
            kept = kept + jnp.where(self.before(self.ctx, i), arrived, 0.0)
        self.total[...] = total
        self.kept[...] = kept
        for i in range(1, self.n_seq):
            self.far_copy(i).start()

    def result(self):
        kept = self.kept[...]
        for i in range(1, self.n_seq):
            self.far_copy(i).wait_recv()
            kept = kept + jnp.where(self.before(self.seq, i), self.far[i - 1], 0.0)
        return kept

    def finish(self):
        for i in range(1, self.n_ctx):
            self.near_copy(i).wait_send()
        for i in range(1, self.n_seq):
            self.far_copy(i).wait_send()


def radices(pairs):
    out = []
    while pairs > 1:
        out.append(4 if pairs % 4 == 0 else 2)
        pairs //= out[-1]
    return out


class Scan:
    def __init__(self, n_ctx, n_seq, reverse, refs):
        (
            self.x, self.total, self.peer, self.part, self.got, self.before,
            self.up, self.up_got, self.down, self.down_got, self.send_sem, self.recv_sem,
        ) = refs
        ctx, seq = lax.axis_index("ctx"), lax.axis_index("seq")
        step = -1 if reverse else 1
        self.step, self.ctx, self.seq = step, ctx, seq
        self.n_ctx = n_ctx
        self.place = n_ctx - 1 - ctx if reverse else ctx
        line = n_seq - 1 - seq if reverse else seq
        self.mine = line % 2
        self.radices = radices(n_seq // 2)
        self.digits, self.strides, self.slots = [], [], []
        stride = slot = 0
        stride = 1
        for radix in self.radices:
            self.digits.append((line // 2 // stride) % radix)
            self.strides.append(stride)
            self.slots.append(slot)
            stride, slot = stride * radix, slot + radix - 1
        self.n_slots = slot
        self.has_above = self.place < n_ctx - 1
        self.has_below = self.place > 0
        self.above = (lax.rem(ctx + step + n_ctx, n_ctx), seq)
        self.below = (lax.rem(ctx - step + n_ctx, n_ctx), seq)
        self.core = (ctx, seq + step * (1 - 2 * self.mine))

    def rows(self, half):
        return pl.ds(pl.multiple_of(half * HALF, HALF), HALF)

    def copy(self, n, c, source, target, device):
        return pltpu.make_async_remote_copy(
            src_ref=source,
            dst_ref=target,
            send_sem=self.send_sem.at[n, c],
            recv_sem=self.recv_sem.at[n, c],
            device_id=device,
            device_id_type=MESH,
        )

    def upward(self, c):
        return self.copy(0, c, self.up.at[c], self.up_got.at[c], self.above)

    def downward(self, c):
        return self.copy(1, c, self.down.at[c], self.down_got.at[c], self.below)

    def swap(self, c):
        return self.copy(2, c, self.total.at[c], self.peer.at[c], self.core)

    def share(self, c):
        half = self.rows(self.mine)
        return self.copy(3, c, self.before.at[c, half], self.before.at[c, half], self.core)

    def exchange(self, r, i, c):
        radix, digit, stride = self.radices[r], self.digits[r], self.strides[r]
        move = (lax.rem(digit + i, radix) - digit) * stride * 2
        slot = self.slots[r] + i - 1
        return self.copy(
            4 + slot, c, self.part.at[r, c], self.got.at[slot, c], (self.ctx, self.seq + self.step * move)
        )

    def sends(self, r, i):
        return self.digits[r] + i < self.radices[r] if r == len(self.radices) - 1 else None

    def gets(self, r, i):
        return self.digits[r] >= i if r == len(self.radices) - 1 else None

    def guarded(self, condition, action):
        if condition is None:
            action()
        else:
            pl.when(condition)(action)

    def send_part(self, r, c):
        for i in range(1, self.radices[r]):
            self.guarded(self.sends(r, i), lambda i=i: self.exchange(r, i, c).start())

    def pair(self, c):
        self.swap(c).wait_recv()
        half = self.rows(self.mine)
        self.part[0, c] = self.total[c, half] + self.peer[c, half]
        self.send_part(0, c)

    def round(self, r, c):
        last = r == len(self.radices) - 1
        kept = jnp.zeros((HALF, LANES), F32)
        if r:
            kept = self.before[c, self.rows(self.mine)]
        total = None if last else self.part[r, c]
        for i in range(1, self.radices[r]):
            self.guarded(self.gets(r, i), lambda i=i: self.exchange(r, i, c).wait_recv())
            arrived = self.got[self.slots[r] + i - 1, c]
            kept = kept + jnp.where(self.digits[r] >= i, arrived, 0.0)
            if not last:
                total = total + arrived
        self.before[c, self.rows(self.mine)] = kept
        if last:
            self.share(c).start()
        else:
            self.part[r + 1, c] = total
            self.send_part(r + 1, c)

    def outer(self, c):
        return self.before[c] + jnp.where(self.mine == 1, self.peer[c], 0.0)

    def add_up(self, c, base, first):
        if first:
            @pl.when(self.has_above & ~self.has_below)
            def _():
                self.up[c] = base
                self.upward(c).start()

    def finish(self, c):
        self.swap(c).wait_send()
        self.share(c).wait_send()
        for r in range(len(self.radices)):
            for i in range(1, self.radices[r]):
                self.guarded(self.sends(r, i), lambda r=r, i=i: self.exchange(r, i, c).wait_send())

        @pl.when(self.has_below)
        def _():
            self.downward(c).wait_send()

        @pl.when(self.has_above)
        def _():
            self.upward(c).wait_send()


class Inner(Scan):
    def begin(self, c, state):
        self.x[c] = state

        @pl.when(self.has_above & ~self.has_below)
        def _():
            self.up[c] = state
            self.upward(c).start()

        @pl.when(self.has_below & ~self.has_above)
        def _():
            self.down[c] = state
            self.downward(c).start()

    def rise(self, c):
        self.upward(c).wait_recv()

        @pl.when(self.has_above)
        def _():
            self.up[c] = self.x[c] + self.up_got[c]
            self.upward(c).start()

    def sink(self, c):
        self.downward(c).wait_recv()

        @pl.when(self.has_below)
        def _():
            self.down[c] = self.x[c] + self.down_got[c]
            self.downward(c).start()

    def whole(self, c):
        total = self.x[c] + jnp.where(self.has_below, self.up_got[c], 0.0)
        self.total[c] = total + jnp.where(self.has_above, self.down_got[c], 0.0)
        self.swap(c).start()

    def joined(self, c):
        self.share(c).wait_recv()

    def result(self, c):
        return self.outer(c) + jnp.where(self.has_below, self.up_got[c], 0.0)

    def stages(self, start, lags):
        pair_lag, round_lag, share_lag, hop_lag = lags
        n = self.n_ctx - 1
        out = [
            (self.rise, start + hop_lag * self.place, self.has_below),
            (self.sink, start + hop_lag * (n - self.place), self.has_above),
        ]
        at = start + hop_lag * n
        out.append((self.whole, start + hop_lag * jnp.maximum(self.place, n - self.place), None))
        at += pair_lag
        out.append((self.pair, at, None))
        for r in range(len(self.radices)):
            at += round_lag
            out.append((functools.partial(self.round, r), at, None))
        at += share_lag
        out.append((self.joined, at, None))
        return out, at


class Outer(Scan):
    def begin(self, c, state):
        self.total[c] = state
        self.swap(c).start()

    def joined(self, c):
        self.share(c).wait_recv()

        @pl.when(self.has_above & ~self.has_below)
        def _():
            self.up[c] = self.outer(c) + self.total[c]
            self.upward(c).start()

        @pl.when(self.has_below & ~self.has_above)
        def _():
            self.down[c] = self.outer(c)
            self.downward(c).start()

    def rise(self, c):
        self.upward(c).wait_recv()

        @pl.when(self.has_above)
        def _():
            self.up[c] = self.outer(c) + self.total[c] + self.up_got[c]
            self.upward(c).start()

    def sink(self, c):
        self.downward(c).wait_recv()

        @pl.when(self.has_below)
        def _():
            self.down[c] = self.outer(c) + self.down_got[c]
            self.downward(c).start()

    def result(self, c):
        total = self.outer(c) + jnp.where(self.has_below, self.up_got[c], 0.0)
        return total + jnp.where(self.has_above, self.down_got[c], 0.0)

    def stages(self, start, lags):
        pair_lag, round_lag, share_lag, hop_lag = lags
        n = self.n_ctx - 1
        at = start + pair_lag
        out = [(self.pair, at, None)]
        for r in range(len(self.radices)):
            at += round_lag
            out.append((functools.partial(self.round, r), at, None))
        at += share_lag
        out.append((self.joined, at, None))
        out.append((self.rise, at + hop_lag * self.place, self.has_below))
        out.append((self.sink, at + hop_lag * (n - self.place), self.has_above))
        return out, at + hop_lag * n


SMALL_REFS = 7
SCAN_REFS = 12
LAGS = (1, 3, 1, 3)
LATE_LAGS = (1, 3, 1, 3)
NORM_TURN = 3
NORM_DONE = 8
SHARE_LAG = 3


def kernel(
    n_ctx, n_seq, q_ref, k_ref, v_ref, g_ref, out_ref, gq_ref, gk_ref, gv_ref,
    qt, kt, qt16, kt16, den, rden, shares, yn, numer, gv_acc, gqt, gkt, phik, phiq, *refs,
):
    norms = Small(n_ctx, n_seq, False, refs[:SMALL_REFS])
    pulls = Small(n_ctx, n_seq, True, refs[SMALL_REFS : 2 * SMALL_REFS])
    refs = refs[2 * SMALL_REFS :]
    earlier = Inner(n_ctx, n_seq, False, refs[:SCAN_REFS])
    later = Outer(n_ctx, n_seq, True, refs[SCAN_REFS:])
    ctx, seq = norms.ctx, norms.seq
    length = q_ref.shape[0]
    scale = 1.0 / math.sqrt(QK_DIM)

    barrier = pltpu.get_barrier_semaphore()
    for i in range(1, n_ctx):
        pl.semaphore_signal(
            barrier, inc=1, device_id=(lax.rem(ctx + i, n_ctx), seq), device_id_type=MESH
        )
    for i in range(1, n_seq):
        pl.semaphore_signal(
            barrier, inc=1, device_id=(ctx, lax.rem(seq + i, n_seq)), device_id_type=MESH
        )

    def wide(head):
        return pl.ds(pl.multiple_of(head * HEAD_DIM, HEAD_DIM), HEAD_DIM)

    def narrow(head):
        return pl.ds(pl.multiple_of(head * QK_DIM, QK_DIM), QK_DIM)

    def one(head):
        return pl.ds(head, 1)

    def indicator():
        return jnp.where(
            iota((HEADS, LANES), 1) // QK_DIM == iota((HEADS, LANES), 0), 1.0, 0.0
        ).astype(BF16)

    def causal():
        return iota((length, length), 0) <= iota((length, length), 1)

    def scores(head):
        return dot(kt16[narrow(head), :], qt16[narrow(head), :], TN)

    def kernel_of(s):
        return jnp.where(causal(), 1.0 + s + 0.5 * s * s, 0.0)

    q32, k32 = q_ref[...].astype(F32), k_ref[...].astype(F32)
    qt[...] = q32.T
    kt[...] = k32.T
    qt16[...] = (qt[...] * scale).astype(BF16)
    kt16[...] = kt[...].astype(BF16)
    norms.own[0:QK_DIM, :] = compact(dot(k_ref[...], k_ref[...], TN))
    norms.own[QK_DIM:, :] = dot(jnp.ones((8, length), BF16), k_ref[...])

    pl.semaphore_wait(barrier, n_ctx + n_seq - 2)
    norms.start()

    def key_state(head):
        high, low = split(features(kt[narrow(head), :]))
        phik[head, 0:ROWS, :] = high
        phik[head, ROWS : 2 * ROWS, :] = low
        phik[head, 2 * ROWS : 3 * ROWS, :] = high
        earlier.begin(head, dot2((high, low), v_ref[:, wide(head)]))

    def prepare(head):
        kern = kernel_of(scores(head))
        den[one(head), :] = jnp.sum(kern, axis=0, keepdims=True)
        numer[head] = dot2r(v_ref[:, wide(head)], split(kern), TN)

    def norm_turn(_):
        norms.turn()

    def norm_done(_):
        prior = norms.result()
        square = split(blocks(prior[:QK_DIM]))
        linear = prior[QK_DIM : QK_DIM + 1, :] * scale
        y = dot2r(q_ref[...], square)
        yn[...] = y * (scale * scale) + linear
        z = q_ref[...].astype(F32) * (y * (0.5 * scale * scale) + linear)
        count = (length * (seq * n_ctx + ctx)).astype(F32)
        rden[...] = 1.0 / (den[...] + dot2r(indicator(), split(z), NT) + count)

    def query_state(head):
        phi = features(qt[narrow(head), :])
        high, low = split(phi)
        phiq[head, 0:ROWS, :] = high
        phiq[head, ROWS : 2 * ROWS, :] = low
        phiq[head, 2 * ROWS : 3 * ROWS, :] = high
        later.begin(head, dot2(split(phi * rden[one(head), :]), g_ref[:, wide(head)]))

    def local_values(head):
        kern = kernel_of(scores(head)) * rden[one(head), :]
        gv_acc[head] = dot2(split(kern), g_ref[:, wide(head)])

    def middle(head):
        g = g_ref[:, wide(head)]
        high, low = split(weighed(earlier.result(head)))
        row = rden[one(head), :]
        state = jnp.concatenate([high, high, low], axis=0)
        out = (numer[head] + dot(state, phiq[head], TN)) * row
        out_ref[:, wide(head)] = out.T.astype(BF16)
        share = jnp.sum(g.astype(F32).T * out, axis=0, keepdims=True) * row
        shares[one(head), :] = share
        grad = dot(jnp.concatenate([high, low], axis=1), jnp.concatenate([g, g], axis=1), NT)
        gqt[narrow(head), :] = pull(grad, qt[narrow(head), :]) * row

    def local_gradients(head):
        s = scores(head)
        direct = dot(v_ref[:, wide(head)], g_ref[:, wide(head)], NT)
        direct = direct * rden[one(head), :] - shares[one(head), :]
        grad = split(jnp.where(causal(), direct * (1.0 + s), 0.0))
        gqt[narrow(head), :] += dot2r(kt16[narrow(head), :], grad) * scale
        gkt[narrow(head), :] = dot2r(qt16[narrow(head), :], grad, NT)

    def share_start(_):
        spread = dot2(split(shares[...]), indicator(), TN)
        gq_ref[...] = (gqt[...].T - spread * yn[...]).astype(BF16)
        part = split(q_ref[...].astype(F32) * spread)
        pulls.own[0:QK_DIM, :] = compact(dot2r(q_ref[...], part, TN))
        pulls.own[QK_DIM:, :] = dot2r(jnp.ones((8, length), BF16), part)
        pulls.start()

    def share_turn(_):
        pulls.turn()

    def last(head):
        v = v_ref[:, wide(head)]
        high, low = split(weighed(later.result(head)))
        state = jnp.concatenate([high, high, low], axis=0)
        grad_v = gv_acc[head] + dot(phik[head], state, TN)
        gv_ref[:, wide(head)] = grad_v.astype(BF16)
        grad = dot(jnp.concatenate([high, low], axis=1), jnp.concatenate([v, v], axis=1), NT)
        gkt[narrow(head), :] += pull(grad, kt[narrow(head), :])

    early_stages, early_done = earlier.stages(0, LAGS)
    late_stages, late_done = later.stages(NORM_DONE, LATE_LAGS)
    share_at = early_done + HEADS
    end = max(late_done + HEADS, share_at + SHARE_LAG + 1)
    plan = [stage + (HEADS,) for stage in early_stages + late_stages] + [
        (key_state, 0, None, HEADS),
        (norm_turn, NORM_TURN, None, 1),
        (prepare, 0, None, HEADS),
        (norm_done, NORM_DONE, None, 1),
        (query_state, NORM_DONE, None, HEADS),
        (local_values, NORM_DONE, None, HEADS),
        (middle, early_done, None, HEADS),
        (local_gradients, early_done, None, HEADS),
        (share_start, share_at, None, 1),
        (share_turn, share_at + SHARE_LAG, None, 1),
        (last, late_done, None, HEADS),
    ]

    def turn(t, carry):
        for body, start, condition, count in plan:
            head = t - start
            ok = (head >= 0) & (head < count)

            @pl.when(ok if condition is None else ok & condition)
            def _(body=body, head=head):
                body(head)

        return carry

    lax.fori_loop(0, end, turn, 0)
    after = pulls.result()
    square = split(blocks(after[:QK_DIM]))
    norm = dot2r(k_ref[...], square) * (scale * scale) + after[QK_DIM : QK_DIM + 1, :] * scale
    gk_ref[...] = (gkt[...].T - norm).astype(BF16)

    def finish(c, carry):
        earlier.finish(c)
        later.finish(c)
        return carry

    lax.fori_loop(0, HEADS, finish, 0)
    norms.finish()
    pulls.finish()


def deliver(*refs):
    sem = refs[8]
    copies = [pltpu.make_async_copy(refs[i], refs[4 + i], sem.at[i]) for i in range(4)]
    for copy in copies:
        copy.start()
    for copy in copies:
        copy.wait()


def small_refs(n_ctx, n_seq):
    rows = QK_DIM + 8
    one = pltpu.VMEM((rows, LANES), F32)
    semaphores = pltpu.SemaphoreType.DMA((n_ctx + n_seq - 2,))
    return [
        one, pltpu.VMEM((n_ctx - 1, rows, LANES), F32), one, one,
        pltpu.VMEM((n_seq - 1, rows, LANES), F32), semaphores, semaphores,
    ]


def scan_refs(n_seq):
    rounds = radices(n_seq // 2)
    slots = sum(rounds) - len(rounds)
    full = pltpu.VMEM((HEADS, ROWS, LANES), F32)
    parts = pltpu.VMEM((len(rounds), HEADS, HALF, LANES), F32)
    halves = pltpu.VMEM((slots, HEADS, HALF, LANES), F32)
    semaphores = pltpu.SemaphoreType.DMA((slots + 4, HEADS))
    return [full, full, full, parts, halves, full, full, full, full, full, semaphores, semaphores]


def per_device(n_ctx, n_seq, queries, keys, values, grad_output):
    length = queries.shape[0]
    across = pltpu.VMEM((LANES, length), F32)
    across16 = pltpu.VMEM((LANES, length), BF16)
    rows = pltpu.VMEM((HEADS, length), F32)
    stacked = pltpu.VMEM((HEADS, 3 * ROWS, length), BF16)
    scratch = [
        across, across, across16, across16, rows, rows, rows,
        pltpu.VMEM((length, LANES), F32),
        pltpu.VMEM((HEADS, HEAD_DIM, length), F32),
        pltpu.VMEM((HEADS, length, HEAD_DIM), F32),
        across, across, stacked, stacked,
    ]
    scratch += small_refs(n_ctx, n_seq) * 2 + scan_refs(n_seq) * 2
    vmem = pl.BlockSpec(memory_space=pltpu.VMEM)
    results = pl.pallas_call(
        functools.partial(kernel, n_ctx, n_seq),
        out_shape=(
            jax.ShapeDtypeStruct(values.shape, BF16),
            jax.ShapeDtypeStruct(queries.shape, BF16),
            jax.ShapeDtypeStruct(keys.shape, BF16),
            jax.ShapeDtypeStruct(values.shape, BF16),
        ),
        in_specs=[vmem] * 4,
        out_specs=(vmem,) * 4,
        scratch_shapes=scratch,
        compiler_params=pltpu.CompilerParams(
            collective_id=0, has_side_effects=True, vmem_limit_bytes=56 << 20
        ),
        name="attention",
    )(queries, keys, values, grad_output)
    anywhere = pl.BlockSpec(memory_space=pl.ANY)
    inside = pl.BlockSpec(memory_space=pltpu.VMEM)
    return pl.pallas_call(
        deliver,
        out_shape=tuple(jax.ShapeDtypeStruct(a.shape, a.dtype) for a in results),
        in_specs=[inside] * 4,
        out_specs=(anywhere,) * 4,
        scratch_shapes=[pltpu.SemaphoreType.DMA((4,))],
        name="deliver",
    )(*results)


def solution(mesh):
    placed = P(("seq", "ctx"), None)
    return jax.shard_map(
        functools.partial(per_device, mesh.shape["ctx"], mesh.shape["seq"]),
        mesh=mesh,
        in_specs=(placed,) * 4,
        out_specs=(placed,) * 4,
        check_vma=False,
    )
```

```python
import functools
import math

import jax
import jax.numpy as jnp
from jax import lax
from jax.experimental import pallas as pl
from jax.experimental.pallas import tpu as pltpu
from jax.sharding import PartitionSpec as P

HEADS = 8
QK_DIM = 16
HEAD_DIM = 128
LANES = 128
ROWS = 160
HALF = ROWS // 2
PIECES = 2
CHUNKS = HEADS * PIECES
PIECE = ROWS // PIECES
MESH = pl.DeviceIdType.MESH
NN = (((1,), (0,)), ((), ()))
NT = (((1,), (1,)), ((), ()))
TN = (((0,), (0,)), ((), ()))
F32 = jnp.float32
BF16 = jnp.bfloat16


def dot(a, b, dims=NN):
    return lax.dot_general(a, b, dims, preferred_element_type=F32)


def split(x):
    high = x.astype(BF16)
    return high, (x - high.astype(F32)).astype(BF16)


def dot2(pair, b, dims=NN):
    return dot(pair[0], b, dims) + dot(pair[1], b, dims)


def dot2r(a, pair, dims=NN):
    return dot(a, pair[0], dims) + dot(a, pair[1], dims)


def iota(shape, dim):
    return lax.broadcasted_iota(jnp.int32, shape, dim)


def shifted(x, d):
    return pltpu.roll(x, d % QK_DIM, 0)


def features(x):
    half = QK_DIM // 2
    parts = [x, x * x]
    for d in range(1, half):
        parts.append(x * shifted(x, -d))
    parts.append(x[:half] * x[half:])
    parts.append(jnp.where(iota((8, x.shape[1]), 0) == 0, 1.0, 0.0))
    return jnp.concatenate(parts, axis=0)


def weighed(state):
    w = QK_DIM
    last = ROWS - 8
    return jnp.concatenate(
        [
            state[:w] * (1.0 / math.sqrt(w)),
            state[w : 2 * w] * (0.5 / w),
            state[2 * w : last] * (1.0 / w),
            state[last:],
        ],
        axis=0,
    )


def pull(grad, x):
    w, half = QK_DIM, QK_DIM // 2
    total = grad[:w] + 2.0 * grad[w : 2 * w] * x
    for d in range(1, half):
        rows = grad[w * (d + 1) : w * (d + 2)]
        total = total + rows * shifted(x, -d) + shifted(rows * x, d)
    rows = grad[w * (half + 1) : w * (half + 1) + half]
    return total + jnp.concatenate([rows * x[half:], rows * x[:half]], axis=0)


def own_block():
    return iota((LANES, LANES), 0) // QK_DIM == iota((LANES, LANES), 1) // QK_DIM


def compact(square):
    kept = jnp.where(own_block(), square, 0.0)
    total = kept[:QK_DIM]
    for h in range(1, HEADS):
        total = total + kept[h * QK_DIM : (h + 1) * QK_DIM]
    return total


def blocks(rows):
    return jnp.where(own_block(), jnp.concatenate([rows] * HEADS, axis=0), 0.0)


class Small:
    def __init__(self, n_ctx, n_seq, reverse, refs):
        self.own, self.got, self.total, self.kept, self.far, self.send_sem, self.recv_sem = refs
        self.n_ctx, self.n_seq, self.reverse = n_ctx, n_seq, reverse
        self.ctx, self.seq = lax.axis_index("ctx"), lax.axis_index("seq")

    def copy(self, source, target, n, device):
        return pltpu.make_async_remote_copy(
            src_ref=source,
            dst_ref=target,
            send_sem=self.send_sem.at[n],
            recv_sem=self.recv_sem.at[n],
            device_id=device,
            device_id_type=MESH,
        )

    def near_to(self, i):
        return (lax.rem(self.ctx + i, self.n_ctx), self.seq)

    def far_to(self, i):
        return (self.ctx, lax.rem(self.seq + i, self.n_seq))

    def near_all(self):
        return self.copy(self.got, self.got, 0, self.near_to(1))

    def far_all(self):
        return self.copy(self.far, self.far, 1, self.far_to(1))

    def before(self, place, i):
        return place < i if self.reverse else place >= i

    def start(self):
        for i in range(1, self.n_ctx):
            self.copy(self.own, self.got.at[i - 1], 0, self.near_to(i)).start()

    def turn(self):
        total = self.own[...]
        kept = jnp.zeros_like(total)
        self.near_all().wait_recv()
        for i in range(1, self.n_ctx):
            arrived = self.got[i - 1]
            total = total + arrived
            kept = kept + jnp.where(self.before(self.ctx, i), arrived, 0.0)
        self.total[...] = total
        self.kept[...] = kept
        for i in range(1, self.n_seq):
            self.copy(self.total, self.far.at[i - 1], 1, self.far_to(i)).start()

    def result(self):
        kept = self.kept[...]
        self.far_all().wait_recv()
        for i in range(1, self.n_seq):
            kept = kept + jnp.where(self.before(self.seq, i), self.far[i - 1], 0.0)
        return kept

    def finish(self):
        self.near_all().wait_send()
        self.far_all().wait_send()


def radices(pairs):
    out = []
    while pairs > 1:
        out.append(4 if pairs % 4 == 0 else 2)
        pairs //= out[-1]
    return out


class Scan:
    def __init__(self, n_ctx, n_seq, reverse, refs):
        (
            self.x, self.total, self.peer, self.part, self.got, self.before,
            self.up, self.up_got, self.down, self.down_got, self.send_sem, self.chain_sem, self.recv_sem,
        ) = refs
        ctx, seq = lax.axis_index("ctx"), lax.axis_index("seq")
        step = -1 if reverse else 1
        self.step, self.ctx, self.seq = step, ctx, seq
        self.n_ctx = n_ctx
        self.place = n_ctx - 1 - ctx if reverse else ctx
        line = n_seq - 1 - seq if reverse else seq
        self.mine = line % 2
        self.radices = radices(n_seq // 2)
        self.digits, self.strides, self.slots = [], [], []
        stride = slot = 0
        stride = 1
        for radix in self.radices:
            self.digits.append((line // 2 // stride) % radix)
            self.strides.append(stride)
            self.slots.append(slot)
            stride, slot = stride * radix, slot + radix - 1
        self.n_slots = slot
        self.has_above = self.place < n_ctx - 1
        self.has_below = self.place > 0
        self.above = (lax.rem(ctx + step + n_ctx, n_ctx), seq)
        self.below = (lax.rem(ctx - step + n_ctx, n_ctx), seq)
        self.core = (ctx, seq + step * (1 - 2 * self.mine))

    def rows(self, half):
        return pl.ds(pl.multiple_of(half * HALF, HALF), HALF)

    def piece(self, c):
        return c // PIECES, pl.ds(pl.multiple_of(c % PIECES * PIECE, PIECE), PIECE)

    def copy(self, n, receive, source, target, device):
        return pltpu.make_async_remote_copy(
            src_ref=source,
            dst_ref=target,
            send_sem=self.send_sem.at[n],
            recv_sem=receive,
            device_id=device,
            device_id_type=MESH,
        )

    def upward(self, c):
        at = self.piece(c)
        return self.copy(0, self.chain_sem.at[0, c], self.up.at[at], self.up_got.at[at], self.above)

    def downward(self, c):
        at = self.piece(c)
        return self.copy(
            1, self.chain_sem.at[1, c], self.down.at[at], self.down_got.at[at], self.below
        )

    def swap(self, c):
        return self.copy(2, self.recv_sem.at[0, c], self.total.at[c], self.peer.at[c], self.core)

    def share(self, c):
        half = self.before.at[c, self.rows(self.mine)]
        return self.copy(3, self.recv_sem.at[1, c], half, half, self.core)

    def exchange(self, r, i, c):
        radix, digit, stride = self.radices[r], self.digits[r], self.strides[r]
        move = (lax.rem(digit + i, radix) - digit) * stride * 2
        slot = self.slots[r] + i - 1
        return self.copy(
            4 + slot, self.recv_sem.at[2 + r, c], self.part.at[r, c], self.got.at[slot, c],
            (self.ctx, self.seq + self.step * move),
        )

    def arrive(self, r, c):
        def wait(n):
            slots = self.got.at[self.slots[r] : self.slots[r] + n, c]
            self.copy(4, self.recv_sem.at[2 + r, c], slots, slots, self.core).wait_recv()

        radix = self.radices[r]
        if r < len(self.radices) - 1:
            wait(radix - 1)
        else:
            for n in range(1, radix):
                pl.when(self.digits[r] == n)(functools.partial(wait, n))

    def sends(self, r, i):
        return self.digits[r] + i < self.radices[r] if r == len(self.radices) - 1 else None

    def guarded(self, condition, action):
        if condition is None:
            action()
        else:
            pl.when(condition)(action)

    def send_part(self, r, c):
        for i in range(1, self.radices[r]):
            self.guarded(self.sends(r, i), lambda i=i: self.exchange(r, i, c).start())

    def pair(self, c):
        self.swap(c).wait_recv()
        half = self.rows(self.mine)
        self.part[0, c] = self.total[c, half] + self.peer[c, half]
        self.send_part(0, c)

    def round(self, r, c):
        last = r == len(self.radices) - 1
        kept = jnp.zeros((HALF, LANES), F32)
        if r:
            kept = self.before[c, self.rows(self.mine)]
        total = None if last else self.part[r, c]
        self.arrive(r, c)
        for i in range(1, self.radices[r]):
            arrived = self.got[self.slots[r] + i - 1, c]
            kept = kept + jnp.where(self.digits[r] >= i, arrived, 0.0)
            if not last:
                total = total + arrived
        self.before[c, self.rows(self.mine)] = kept
        if last:
            self.share(c).start()
        else:
            self.part[r + 1, c] = total
            self.send_part(r + 1, c)

    def outer(self, c):
        return self.before[c] + jnp.where(self.mine == 1, self.peer[c], 0.0)

    def sent(self, n, source, target):
        self.copy(n, self.recv_sem.at[0, 0], source, target, self.core).wait_send()

    def finish(self):
        self.sent(2, self.total, self.peer)
        half = self.rows(self.mine)
        self.sent(3, self.before.at[:, half], self.before.at[:, half])
        for r in range(len(self.radices)):
            for i in range(1, self.radices[r]):
                slot = self.slots[r] + i - 1
                self.guarded(
                    self.sends(r, i),
                    lambda r=r, slot=slot: self.sent(4 + slot, self.part.at[r], self.got.at[slot]),
                )

        @pl.when(self.has_below)
        def _():
            self.sent(1, self.down, self.down_got)

        @pl.when(self.has_above)
        def _():
            self.sent(0, self.up, self.up_got)


class Inner(Scan):
    def put(self, head, state):
        self.x[head] = state
        self.up[head] = state
        self.down[head] = state

    def begin(self, c):
        @pl.when(self.has_above & ~self.has_below)
        def _():
            self.upward(c).start()

        @pl.when(self.has_below & ~self.has_above)
        def _():
            self.downward(c).start()

    def rise(self, c):
        self.upward(c).wait_recv()

        @pl.when(self.has_above)
        def _():
            at = self.piece(c)
            self.up[at] = self.x[at] + self.up_got[at]
            self.upward(c).start()

    def sink(self, c):
        self.downward(c).wait_recv()

        @pl.when(self.has_below)
        def _():
            at = self.piece(c)
            self.down[at] = self.x[at] + self.down_got[at]
            self.downward(c).start()

    def whole(self, c):
        total = self.x[c] + jnp.where(self.has_below, self.up_got[c], 0.0)
        self.total[c] = total + jnp.where(self.has_above, self.down_got[c], 0.0)
        self.swap(c).start()

    def joined(self, c):
        self.share(c).wait_recv()

    def result(self, c):
        return self.outer(c) + jnp.where(self.has_below, self.up_got[c], 0.0)

    def stages(self, start, lags):
        pair_lag, round_lag, share_lag, hop_lag = lags
        n = self.n_ctx - 1
        out = [
            (self.rise, start + hop_lag * self.place, 1, CHUNKS, self.has_below),
            (self.sink, start + hop_lag * (n - self.place), 1, CHUNKS, self.has_above),
        ]
        at = start + PIECES - 1 + hop_lag * n
        middle = start + PIECES - 1 + hop_lag * jnp.maximum(self.place, n - self.place)
        out.append((self.whole, middle, PIECES, HEADS, None))
        at += pair_lag
        out.append((self.pair, at, PIECES, HEADS, None))
        for r in range(len(self.radices)):
            at += round_lag
            out.append((functools.partial(self.round, r), at, PIECES, HEADS, None))
        at += share_lag
        out.append((self.joined, at, PIECES, HEADS, None))
        return out, at


class Outer(Scan):
    def begin(self, head, state):
        self.total[head] = state
        self.swap(head).start()

    def joined(self, c):
        self.share(c).wait_recv()

        @pl.when(self.has_above & ~self.has_below)
        def _():
            self.up[c] = self.outer(c) + self.total[c]
            for p in range(PIECES):
                self.upward(c * PIECES + p).start()

        @pl.when(self.has_below & ~self.has_above)
        def _():
            self.down[c] = self.outer(c)
            for p in range(PIECES):
                self.downward(c * PIECES + p).start()

    def rise(self, c):
        self.upward(c).wait_recv()

        @pl.when(self.has_above)
        def _():
            at = self.piece(c)
            self.up[at] = self.outer(at) + self.total[at] + self.up_got[at]
            self.upward(c).start()

    def sink(self, c):
        self.downward(c).wait_recv()

        @pl.when(self.has_below)
        def _():
            at = self.piece(c)
            self.down[at] = self.outer(at) + self.down_got[at]
            self.downward(c).start()

    def result(self, c):
        total = self.outer(c) + jnp.where(self.has_below, self.up_got[c], 0.0)
        return total + jnp.where(self.has_above, self.down_got[c], 0.0)

    def stages(self, start, lags):
        pair_lag, round_lag, share_lag, hop_lag = lags
        n = self.n_ctx - 1
        at = start + pair_lag
        out = [(self.pair, at, PIECES, HEADS, None)]
        for r in range(len(self.radices)):
            at += round_lag
            out.append((functools.partial(self.round, r), at, PIECES, HEADS, None))
        at += share_lag
        out.append((self.joined, at, PIECES, HEADS, None))
        out.append((self.rise, at + hop_lag * self.place, 1, CHUNKS, self.has_below))
        out.append((self.sink, at + hop_lag * (n - self.place), 1, CHUNKS, self.has_above))
        return out, at + hop_lag * n + PIECES - 1


SMALL_REFS = 7
SCAN_REFS = 13
LAGS = (1, 4, 1, 5)
LATE_LAGS = (2, 5, 1, 5)
EARLY = -3
NORM_TURN = 2
NORM_DONE = 5
LATE = 6
MIDDLE = 0
SHARE_LAG = 3
DELIVER = 2


def kernel(
    n_ctx, n_seq, q_in, k_in, v_in, g_in, out_to, gq_to, gk_to, gv_to,
    q_ref, k_ref, v_ref, g_ref, out_ref, gq_ref, gk_ref, gv_ref, move_sem, qt, kt, qt16, kt16, den, rden, shares, yn, numer, gv_acc, gqt, gkt, phik, phiq, *refs,
):
    norms = Small(n_ctx, n_seq, False, refs[:SMALL_REFS])
    pulls = Small(n_ctx, n_seq, True, refs[SMALL_REFS : 2 * SMALL_REFS])
    refs = refs[2 * SMALL_REFS :]
    earlier = Inner(n_ctx, n_seq, False, refs[:SCAN_REFS])
    later = Outer(n_ctx, n_seq, True, refs[SCAN_REFS:])
    ctx, seq = norms.ctx, norms.seq
    length = q_ref.shape[0]
    scale = 1.0 / math.sqrt(QK_DIM)

    barrier = pltpu.get_barrier_semaphore()
    for i in range(1, n_ctx):
        pl.semaphore_signal(
            barrier, inc=1, device_id=(lax.rem(ctx + i, n_ctx), seq), device_id_type=MESH
        )
    for i in range(1, n_seq):
        pl.semaphore_signal(
            barrier, inc=1, device_id=(ctx, lax.rem(seq + i, n_seq)), device_id_type=MESH
        )

    def wide(head):
        return pl.ds(pl.multiple_of(head * HEAD_DIM, HEAD_DIM), HEAD_DIM)

    def narrow(head):
        return pl.ds(pl.multiple_of(head * QK_DIM, QK_DIM), QK_DIM)

    def one(head):
        return pl.ds(head, 1)

    def indicator():
        return jnp.where(
            iota((HEADS, LANES), 1) // QK_DIM == iota((HEADS, LANES), 0), 1.0, 0.0
        ).astype(BF16)

    def causal():
        return iota((length, length), 0) <= iota((length, length), 1)

    def scores(head):
        return dot(kt16[narrow(head), :], qt16[narrow(head), :], TN)

    def kernel_of(s):
        return jnp.where(causal(), 1.0 + s + 0.5 * s * s, 0.0)

    def arrives(n, source, target):
        return pltpu.make_async_copy(source, target, move_sem.at[n])

    loads = [arrives(0, k_in, k_ref), arrives(1, v_in, v_ref), arrives(2, q_in, q_ref), arrives(3, g_in, g_ref)]
    for load in loads:
        load.start()
    half_heads = HEADS // 2 * HEAD_DIM
    stores = [
        arrives(0, out_ref, out_to), arrives(1, gq_ref, gq_to),
        arrives(2, gv_ref.at[:, :half_heads], gv_to.at[:, :half_heads]),
        arrives(3, gv_ref.at[:, half_heads:], gv_to.at[:, half_heads:]), arrives(4, gk_ref, gk_to),
    ]
    loads[0].wait()
    kt[...] = k_ref[...].astype(F32).T
    kt16[...] = kt[...].astype(BF16)
    norms.own[0:QK_DIM, :] = compact(dot(k_ref[...], k_ref[...], TN))
    norms.own[QK_DIM:, :] = dot(jnp.ones((8, length), BF16), k_ref[...])

    def key_state(head, carry):
        high, low = split(features(kt[narrow(head), :]))
        phik[head, 0:ROWS, :] = high
        phik[head, ROWS : 2 * ROWS, :] = low
        phik[head, 2 * ROWS : 3 * ROWS, :] = high
        earlier.put(head, dot2((high, low), v_ref[:, wide(head)]))
        return carry

    def prepare(head, carry):
        kern = kernel_of(scores(head))
        den[one(head), :] = jnp.sum(kern, axis=0, keepdims=True)
        numer[head] = dot2r(v_ref[:, wide(head)], split(kern), TN)
        return carry

    def begin(c, carry):
        earlier.begin(c)
        return carry

    loads[1].wait()
    lax.fori_loop(0, HEADS, key_state, 0)
    pl.semaphore_wait(barrier, n_ctx + n_seq - 2)
    norms.start()
    lax.fori_loop(0, CHUNKS, begin, 0)
    loads[2].wait()
    qt[...] = q_ref[...].astype(F32).T
    qt16[...] = (qt[...] * scale).astype(BF16)
    loads[3].wait()
    lax.fori_loop(0, HEADS, prepare, 0)

    def norm_turn(_):
        norms.turn()

    def norm_done(_):
        prior = norms.result()
        square = split(blocks(prior[:QK_DIM]))
        linear = prior[QK_DIM : QK_DIM + 1, :] * scale
        y = dot2r(q_ref[...], square)
        yn[...] = y * (scale * scale) + linear
        z = q_ref[...].astype(F32) * (y * (0.5 * scale * scale) + linear)
        count = (length * (seq * n_ctx + ctx)).astype(F32)
        rden[...] = 1.0 / (den[...] + dot2r(indicator(), split(z), NT) + count)

    def query_state(head):
        phi = features(qt[narrow(head), :])
        high, low = split(phi)
        phiq[head, 0:ROWS, :] = high
        phiq[head, ROWS : 2 * ROWS, :] = low
        phiq[head, 2 * ROWS : 3 * ROWS, :] = high
        later.begin(head, dot2(split(phi * rden[one(head), :]), g_ref[:, wide(head)]))

    def local_values(head):
        kern = kernel_of(scores(head)) * rden[one(head), :]
        gv_acc[head] = dot2(split(kern), g_ref[:, wide(head)])

    def middle(head):
        g = g_ref[:, wide(head)]
        high, low = split(weighed(earlier.result(head)))
        row = rden[one(head), :]
        state = jnp.concatenate([high, high, low], axis=0)
        out = (numer[head] + dot(state, phiq[head], TN)) * row
        out_ref[:, wide(head)] = out.T.astype(BF16)
        share = jnp.sum(g.astype(F32).T * out, axis=0, keepdims=True) * row
        shares[one(head), :] = share
        grad = dot(jnp.concatenate([high, low], axis=1), jnp.concatenate([g, g], axis=1), NT)
        gqt[narrow(head), :] = pull(grad, qt[narrow(head), :]) * row

    def local_gradients(head):
        s = scores(head)
        direct = dot(v_ref[:, wide(head)], g_ref[:, wide(head)], NT)
        direct = direct * rden[one(head), :] - shares[one(head), :]
        grad = split(jnp.where(causal(), direct * (1.0 + s), 0.0))
        gqt[narrow(head), :] += dot2r(kt16[narrow(head), :], grad) * scale
        gkt[narrow(head), :] = dot2r(qt16[narrow(head), :], grad, NT)

    def share_start(_):
        spread = dot2(split(shares[...]), indicator(), TN)
        gq_ref[...] = (gqt[...].T - spread * yn[...]).astype(BF16)
        part = split(q_ref[...].astype(F32) * spread)
        pulls.own[0:QK_DIM, :] = compact(dot2r(q_ref[...], part, TN))
        pulls.own[QK_DIM:, :] = dot2r(jnp.ones((8, length), BF16), part)
        pulls.start()
        stores[0].start()
        stores[1].start()

    def share_turn(_):
        pulls.turn()

    def last(head):
        v = v_ref[:, wide(head)]
        high, low = split(weighed(later.result(head)))
        state = jnp.concatenate([high, high, low], axis=0)
        grad_v = gv_acc[head] + dot(phik[head], state, TN)
        gv_ref[:, wide(head)] = grad_v.astype(BF16)
        grad = dot(jnp.concatenate([high, low], axis=1), jnp.concatenate([v, v], axis=1), NT)
        gkt[narrow(head), :] += pull(grad, kt[narrow(head), :])

    def values_too(head):
        query_state(head)
        local_values(head)

    def gradients_too(head):
        middle(head)
        local_gradients(head)

    def first_values(_):
        stores[2].start()

    early_stages, early_done = earlier.stages(EARLY, LAGS)
    late_stages, late_done = later.stages(LATE, LATE_LAGS)
    middle_at = early_done + MIDDLE
    share_at = middle_at + CHUNKS - PIECES + 1
    end = max(late_done + CHUNKS - PIECES + 1, share_at + SHARE_LAG + 1)
    plan = early_stages + late_stages + [
        (norm_turn, NORM_TURN, 1, 1, None),
        (norm_done, NORM_DONE, 1, 1, None),
        (values_too, LATE, PIECES, HEADS, None),
        (gradients_too, middle_at, PIECES, HEADS, None),
        (share_start, share_at, 1, 1, None),
        (share_turn, share_at + SHARE_LAG, 1, 1, None),
        (last, late_done, PIECES, HEADS, None),
        (first_values, late_done + CHUNKS // 2, 1, 1, None),
    ]

    def turn(t, carry):
        for body, start, stride, count, condition in plan:
            past = t - start
            item = past // stride
            ok = (past >= 0) & (item < count)
            if stride > 1:
                ok = ok & (past % stride == 0)

            @pl.when(ok if condition is None else ok & condition)
            def _(body=body, item=item):
                body(item)

        return carry

    lax.fori_loop(0, end, turn, 0)
    stores[3].start()
    after = pulls.result()
    square = split(blocks(after[:QK_DIM]))
    norm = dot2r(k_ref[...], square) * (scale * scale) + after[QK_DIM : QK_DIM + 1, :] * scale
    gk_ref[...] = (gkt[...].T - norm).astype(BF16)
    stores[4].start()

    earlier.finish()
    later.finish()
    norms.finish()
    pulls.finish()
    for store in stores:
        store.wait()


def deliver(*refs):
    sem = refs[12]
    loads, stores = [], []
    for i in (0, 3, 1, 2):
        rows = refs[i].shape[0]
        parts = DELIVER if refs[i].shape[1] > LANES else 1
        for p in range(parts):
            at = pl.ds(p * (rows // parts), rows // parts)
            n = len(loads)
            loads.append(pltpu.make_async_copy(refs[i].at[at], refs[8 + i].at[at], sem.at[n]))
            stores.append(pltpu.make_async_copy(refs[8 + i].at[at], refs[4 + i].at[at], sem.at[n]))
    for load in loads:
        load.start()
    for load, store in zip(loads, stores):
        load.wait()
        store.start()
    for store in stores:
        store.wait()


def small_refs(n_ctx, n_seq):
    rows = QK_DIM + 8
    one = pltpu.VMEM((rows, LANES), F32)
    semaphores = pltpu.SemaphoreType.DMA((2,))
    return [
        one, pltpu.VMEM((n_ctx - 1, rows, LANES), F32), one, one,
        pltpu.VMEM((n_seq - 1, rows, LANES), F32), semaphores, semaphores,
    ]


def scan_refs(n_seq):
    rounds = radices(n_seq // 2)
    slots = sum(rounds) - len(rounds)
    full = pltpu.VMEM((HEADS, ROWS, LANES), F32)
    parts = pltpu.VMEM((len(rounds), HEADS, HALF, LANES), F32)
    halves = pltpu.VMEM((slots, HEADS, HALF, LANES), F32)
    send = pltpu.SemaphoreType.DMA((slots + 4,))
    chain = pltpu.SemaphoreType.DMA((2, CHUNKS))
    receive = pltpu.SemaphoreType.DMA((len(rounds) + 2, HEADS))
    return [full, full, full, parts, halves, full, full, full, full, full, send, chain, receive]


def per_device(n_ctx, n_seq, queries, keys, values, grad_output):
    length = queries.shape[0]
    across = pltpu.VMEM((LANES, length), F32)
    across16 = pltpu.VMEM((LANES, length), BF16)
    rows = pltpu.VMEM((HEADS, length), F32)
    stacked = pltpu.VMEM((HEADS, 3 * ROWS, length), BF16)
    narrow, broad = pltpu.VMEM(queries.shape, BF16), pltpu.VMEM(values.shape, BF16)
    scratch = [
        narrow, narrow, broad, broad, broad, narrow, narrow, broad, pltpu.SemaphoreType.DMA((5,)),
        across, across, across16, across16, rows, rows, rows,
        pltpu.VMEM((length, LANES), F32),
        pltpu.VMEM((HEADS, HEAD_DIM, length), F32),
        pltpu.VMEM((HEADS, length, HEAD_DIM), F32),
        across, across, stacked, stacked,
    ]
    scratch += small_refs(n_ctx, n_seq) * 2 + scan_refs(n_seq) * 2
    anywhere = pl.BlockSpec(memory_space=pl.ANY)
    results = pl.pallas_call(
        functools.partial(kernel, n_ctx, n_seq),
        out_shape=(
            jax.ShapeDtypeStruct(values.shape, BF16),
            jax.ShapeDtypeStruct(queries.shape, BF16),
            jax.ShapeDtypeStruct(keys.shape, BF16),
            jax.ShapeDtypeStruct(values.shape, BF16),
        ),
        in_specs=[anywhere] * 4,
        out_specs=(anywhere,) * 4,
        scratch_shapes=scratch,
        compiler_params=pltpu.CompilerParams(
            collective_id=0, has_side_effects=True, vmem_limit_bytes=56 << 20
        ),
        name="attention",
    )(queries, keys, values, grad_output)
    return pl.pallas_call(
        deliver,
        out_shape=tuple(jax.ShapeDtypeStruct(a.shape, a.dtype) for a in results),
        in_specs=[anywhere] * 4,
        out_specs=(anywhere,) * 4,
        scratch_shapes=[pltpu.VMEM(a.shape, a.dtype) for a in results]
        + [pltpu.SemaphoreType.DMA((2 * DELIVER + 2,))],
        name="deliver",
    )(*results)


def solution(mesh):
    placed = P(("seq", "ctx"), None)
    return jax.shard_map(
        functools.partial(per_device, mesh.shape["ctx"], mesh.shape["seq"]),
        mesh=mesh,
        in_specs=(placed,) * 4,
        out_specs=(placed,) * 4,
        check_vma=False,
    )
```

```python
import functools
import math

import jax
import jax.numpy as jnp
from jax import lax
from jax.experimental import pallas as pl
from jax.experimental.pallas import tpu as pltpu
from jax.sharding import PartitionSpec as P

HEADS = 8
QK_DIM = 16
HEAD_DIM = 128
LANES = 128
ROWS = 160
HALF = ROWS // 2
PIECES = 2
CHUNKS = HEADS * PIECES
PIECE = ROWS // PIECES
MESH = pl.DeviceIdType.MESH
NN = (((1,), (0,)), ((), ()))
NT = (((1,), (1,)), ((), ()))
TN = (((0,), (0,)), ((), ()))
F32 = jnp.float32
BF16 = jnp.bfloat16


def dot(a, b, dims=NN):
    return lax.dot_general(a, b, dims, preferred_element_type=F32)


def split(x):
    high = x.astype(BF16)
    return high, (x - high.astype(F32)).astype(BF16)


def dot2(pair, b, dims=NN):
    return dot(pair[0], b, dims) + dot(pair[1], b, dims)


def dot2r(a, pair, dims=NN):
    return dot(a, pair[0], dims) + dot(a, pair[1], dims)


def iota(shape, dim):
    return lax.broadcasted_iota(jnp.int32, shape, dim)


def shifted(x, d):
    return pltpu.roll(x, d % QK_DIM, 0)


def features(x):
    half = QK_DIM // 2
    parts = [x, x * x]
    for d in range(1, half):
        parts.append(x * shifted(x, -d))
    parts.append(x[:half] * x[half:])
    parts.append(jnp.where(iota((8, x.shape[1]), 0) == 0, 1.0, 0.0))
    return jnp.concatenate(parts, axis=0)


def weighed(state):
    w = QK_DIM
    last = ROWS - 8
    return jnp.concatenate(
        [
            state[:w] * (1.0 / math.sqrt(w)),
            state[w : 2 * w] * (0.5 / w),
            state[2 * w : last] * (1.0 / w),
            state[last:],
        ],
        axis=0,
    )


def pull(grad, x):
    w, half = QK_DIM, QK_DIM // 2
    total = grad[:w] + 2.0 * grad[w : 2 * w] * x
    for d in range(1, half):
        rows = grad[w * (d + 1) : w * (d + 2)]
        total = total + rows * shifted(x, -d) + shifted(rows * x, d)
    rows = grad[w * (half + 1) : w * (half + 1) + half]
    return total + jnp.concatenate([rows * x[half:], rows * x[:half]], axis=0)


def own_block():
    return iota((LANES, LANES), 0) // QK_DIM == iota((LANES, LANES), 1) // QK_DIM


def compact(square):
    kept = jnp.where(own_block(), square, 0.0)
    total = kept[:QK_DIM]
    for h in range(1, HEADS):
        total = total + kept[h * QK_DIM : (h + 1) * QK_DIM]
    return total


def blocks(rows):
    return jnp.where(own_block(), jnp.concatenate([rows] * HEADS, axis=0), 0.0)


class Small:
    def __init__(self, n_ctx, n_seq, reverse, refs):
        self.own, self.got, self.total, self.kept, self.far, self.send_sem, self.recv_sem = refs
        self.n_ctx, self.n_seq, self.reverse = n_ctx, n_seq, reverse
        self.ctx, self.seq = lax.axis_index("ctx"), lax.axis_index("seq")

    def copy(self, source, target, n, device):
        return pltpu.make_async_remote_copy(
            src_ref=source,
            dst_ref=target,
            send_sem=self.send_sem.at[n],
            recv_sem=self.recv_sem.at[n],
            device_id=device,
            device_id_type=MESH,
        )

    def near_to(self, i):
        return (lax.rem(self.ctx + i, self.n_ctx), self.seq)

    def far_to(self, i):
        return (self.ctx, lax.rem(self.seq + i, self.n_seq))

    def near_all(self):
        return self.copy(self.got, self.got, 0, self.near_to(1))

    def far_all(self):
        return self.copy(self.far, self.far, 1, self.far_to(1))

    def before(self, place, i):
        return place < i if self.reverse else place >= i

    def start(self):
        for i in range(1, self.n_ctx):
            self.copy(self.own, self.got.at[i - 1], 0, self.near_to(i)).start()

    def turn(self):
        total = self.own[...]
        kept = jnp.zeros_like(total)
        self.near_all().wait_recv()
        for i in range(1, self.n_ctx):
            arrived = self.got[i - 1]
            total = total + arrived
            kept = kept + jnp.where(self.before(self.ctx, i), arrived, 0.0)
        self.total[...] = total
        self.kept[...] = kept
        for i in range(1, self.n_seq):
            self.copy(self.total, self.far.at[i - 1], 1, self.far_to(i)).start()

    def result(self):
        kept = self.kept[...]
        self.far_all().wait_recv()
        for i in range(1, self.n_seq):
            kept = kept + jnp.where(self.before(self.seq, i), self.far[i - 1], 0.0)
        return kept

    def finish(self):
        self.near_all().wait_send()
        self.far_all().wait_send()


def radices(pairs):
    out = []
    while pairs > 1:
        out.append(4 if pairs % 4 == 0 else 2)
        pairs //= out[-1]
    return out


class Scan:
    def __init__(self, n_ctx, n_seq, reverse, first, count, refs):
        self.first, self.count = first, count
        (
            self.x, self.total, self.peer, self.part, self.got, self.before,
            self.up, self.up_got, self.down, self.down_got, self.send_sem, self.chain_sem, self.recv_sem,
        ) = refs
        ctx, seq = lax.axis_index("ctx"), lax.axis_index("seq")
        step = -1 if reverse else 1
        self.step, self.ctx, self.seq = step, ctx, seq
        self.n_ctx = n_ctx
        self.place = n_ctx - 1 - ctx if reverse else ctx
        line = n_seq - 1 - seq if reverse else seq
        self.mine = line % 2
        self.radices = radices(n_seq // 2)
        self.digits, self.strides, self.slots = [], [], []
        stride = slot = 0
        stride = 1
        for radix in self.radices:
            self.digits.append((line // 2 // stride) % radix)
            self.strides.append(stride)
            self.slots.append(slot)
            stride, slot = stride * radix, slot + radix - 1
        self.n_slots = slot
        self.has_above = self.place < n_ctx - 1
        self.has_below = self.place > 0
        self.above = (lax.rem(ctx + step + n_ctx, n_ctx), seq)
        self.below = (lax.rem(ctx - step + n_ctx, n_ctx), seq)
        self.core = (ctx, seq + step * (1 - 2 * self.mine))

    def rows(self, half):
        return pl.ds(pl.multiple_of(half * HALF, HALF), HALF)

    def piece(self, c):
        return c // PIECES, pl.ds(pl.multiple_of(c % PIECES * PIECE, PIECE), PIECE)

    def copy(self, n, receive, source, target, device):
        return pltpu.make_async_remote_copy(
            src_ref=source,
            dst_ref=target,
            send_sem=self.send_sem.at[n],
            recv_sem=receive,
            device_id=device,
            device_id_type=MESH,
        )

    def upward(self, c):
        at = self.piece(c)
        return self.copy(0, self.chain_sem.at[0, c], self.up.at[at], self.up_got.at[at], self.above)

    def downward(self, c):
        at = self.piece(c)
        return self.copy(
            1, self.chain_sem.at[1, c], self.down.at[at], self.down_got.at[at], self.below
        )

    def swap(self, c):
        return self.copy(2, self.recv_sem.at[0, c], self.total.at[c], self.peer.at[c], self.core)

    def share(self, c):
        half = self.before.at[c, self.rows(self.mine)]
        return self.copy(3, self.recv_sem.at[1, c], half, half, self.core)

    def exchange(self, r, i, c):
        radix, digit, stride = self.radices[r], self.digits[r], self.strides[r]
        move = (lax.rem(digit + i, radix) - digit) * stride * 2
        slot = self.slots[r] + i - 1
        return self.copy(
            4 + slot, self.recv_sem.at[2 + r, c], self.part.at[r, c], self.got.at[slot, c],
            (self.ctx, self.seq + self.step * move),
        )

    def arrive(self, r, c):
        def wait(n):
            slots = self.got.at[self.slots[r] : self.slots[r] + n, c]
            self.copy(4, self.recv_sem.at[2 + r, c], slots, slots, self.core).wait_recv()

        radix = self.radices[r]
        if r < len(self.radices) - 1:
            wait(radix - 1)
        else:
            for n in range(1, radix):
                pl.when(self.digits[r] == n)(functools.partial(wait, n))

    def sends(self, r, i):
        return self.digits[r] + i < self.radices[r] if r == len(self.radices) - 1 else None

    def guarded(self, condition, action):
        if condition is None:
            action()
        else:
            pl.when(condition)(action)

    def send_part(self, r, c):
        for i in range(1, self.radices[r]):
            self.guarded(self.sends(r, i), lambda i=i: self.exchange(r, i, c).start())

    def pair(self, c):
        self.swap(c).wait_recv()
        half = self.rows(self.mine)
        self.part[0, c] = self.total[c, half] + self.peer[c, half]
        self.send_part(0, c)

    def round(self, r, c):
        last = r == len(self.radices) - 1
        kept = jnp.zeros((HALF, LANES), F32)
        if r:
            kept = self.before[c, self.rows(self.mine)]
        total = None if last else self.part[r, c]
        self.arrive(r, c)
        for i in range(1, self.radices[r]):
            arrived = self.got[self.slots[r] + i - 1, c]
            kept = kept + jnp.where(self.digits[r] >= i, arrived, 0.0)
            if not last:
                total = total + arrived
        self.before[c, self.rows(self.mine)] = kept
        if last:
            self.share(c).start()
        else:
            self.part[r + 1, c] = total
            self.send_part(r + 1, c)

    def outer(self, c):
        return self.before[c] + jnp.where(self.mine == 1, self.peer[c], 0.0)

    def sent(self, n, source, target):
        self.copy(n, self.recv_sem.at[0, 0], source, target, self.core).wait_send()

    def finish(self):
        mine = pl.ds(self.first, self.count)
        self.sent(2, self.total.at[mine], self.peer.at[mine])
        half = self.before.at[mine, self.rows(self.mine)]
        self.sent(3, half, half)
        for r in range(len(self.radices)):
            for i in range(1, self.radices[r]):
                slot = self.slots[r] + i - 1
                part, got = self.part.at[r, mine], self.got.at[slot, mine]
                self.guarded(
                    self.sends(r, i),
                    lambda slot=slot, part=part, got=got: self.sent(4 + slot, part, got),
                )

        @pl.when(self.has_below)
        def _():
            self.sent(1, self.down.at[mine], self.down_got.at[mine])

        @pl.when(self.has_above)
        def _():
            self.sent(0, self.up.at[mine], self.up_got.at[mine])

    def heads(self, body, start):
        return lambda i: body(i + self.first), start, PIECES, self.count, None

    def chunks(self, body, start, condition):
        return lambda i: body(i + self.first * PIECES), start, 1, self.count * PIECES, condition

    def outer_stages(self, at, lags):
        pair_lag, round_lag, share_lag, _ = lags
        at += pair_lag
        out = [self.heads(self.pair, at)]
        for r in range(len(self.radices)):
            at += round_lag
            out.append(self.heads(functools.partial(self.round, r), at))
        at += share_lag
        out.append(self.heads(self.joined, at))
        return out, at

    def inner_stages(self, at, lags):
        hop_lag, n = lags[3], self.n_ctx - 1
        return [
            self.chunks(self.rise, at + hop_lag * self.place, self.has_below),
            self.chunks(self.sink, at + hop_lag * (n - self.place), self.has_above),
        ]


class Inner(Scan):
    def put(self, head, state):
        self.x[head] = state
        self.up[head] = state
        self.down[head] = state

    def begin(self, head):
        for p in range(PIECES):
            c = head * PIECES + p

            @pl.when(self.has_above & ~self.has_below)
            def _(c=c):
                self.upward(c).start()

            @pl.when(self.has_below & ~self.has_above)
            def _(c=c):
                self.downward(c).start()

    def rise(self, c):
        self.upward(c).wait_recv()

        @pl.when(self.has_above)
        def _():
            at = self.piece(c)
            self.up[at] = self.x[at] + self.up_got[at]
            self.upward(c).start()

    def sink(self, c):
        self.downward(c).wait_recv()

        @pl.when(self.has_below)
        def _():
            at = self.piece(c)
            self.down[at] = self.x[at] + self.down_got[at]
            self.downward(c).start()

    def whole(self, c):
        total = self.x[c] + jnp.where(self.has_below, self.up_got[c], 0.0)
        self.total[c] = total + jnp.where(self.has_above, self.down_got[c], 0.0)
        self.swap(c).start()

    def joined(self, c):
        self.share(c).wait_recv()

    def result(self, c):
        return self.outer(c) + jnp.where(self.has_below, self.up_got[c], 0.0)

    def stages(self, start, lags):
        n = self.n_ctx - 1
        chain = self.inner_stages(start, lags)
        start += PIECES - 1
        whole = self.heads(self.whole, start + lags[3] * jnp.maximum(self.place, n - self.place))
        out, done = self.outer_stages(start + lags[3] * n, lags)
        return chain + [whole] + out, done


class Outer(Scan):
    def put(self, head, state):
        self.total[head] = state

    def begin(self, head):
        self.swap(head).start()

    def joined(self, c):
        self.share(c).wait_recv()

        @pl.when(self.has_above & ~self.has_below)
        def _():
            self.up[c] = self.outer(c) + self.total[c]
            for p in range(PIECES):
                self.upward(c * PIECES + p).start()

        @pl.when(self.has_below & ~self.has_above)
        def _():
            self.down[c] = self.outer(c)
            for p in range(PIECES):
                self.downward(c * PIECES + p).start()

    def rise(self, c):
        self.upward(c).wait_recv()

        @pl.when(self.has_above)
        def _():
            at = self.piece(c)
            self.up[at] = self.outer(at) + self.total[at] + self.up_got[at]
            self.upward(c).start()

    def sink(self, c):
        self.downward(c).wait_recv()

        @pl.when(self.has_below)
        def _():
            at = self.piece(c)
            self.down[at] = self.outer(at) + self.down_got[at]
            self.downward(c).start()

    def result(self, c):
        total = self.outer(c) + jnp.where(self.has_below, self.up_got[c], 0.0)
        return total + jnp.where(self.has_above, self.down_got[c], 0.0)

    def stages(self, start, lags):
        out, at = self.outer_stages(start, lags)
        return out + self.inner_stages(at, lags), at + lags[3] * (self.n_ctx - 1) + PIECES - 1


SMALL_REFS = 7
SCAN_REFS = 13
EARLY = ((Inner, 6, -5, (1, 5, 2, 5)), (Outer, 2, 0, (1, 4, 1, 5)),)
LATE = ((Inner, 3, 10, (1, 7, 2, 5)), (Outer, 5, 7, (2, 5, 1, 5)),)
NORM_TURN = 0
NORM_DONE = 5
SHARE_LAG = 5


def kernel(
    n_ctx, n_seq, q_in, k_in, v_in, g_in, out_ref, gq_ref, gk_ref, gv_ref,
    q_ref, k_ref, v_ref, g_ref, load_sem, qt, kt, qt16, kt16, den, rden, shares, yn, numer, gv_acc, gqt, gkt, phik, phiq, *refs,
):
    norms = Small(n_ctx, n_seq, False, refs[:SMALL_REFS])
    pulls = Small(n_ctx, n_seq, True, refs[SMALL_REFS : 2 * SMALL_REFS])
    refs = refs[2 * SMALL_REFS :]

    def groups(table, reverse, refs):
        out, first = [], 0
        for kind, count, start, lags in table:
            out.append((kind(n_ctx, n_seq, reverse, first, count, refs), start, lags))
            first += count
        return out

    earlier = groups(EARLY, False, refs[:SCAN_REFS])
    later = groups(LATE, True, refs[SCAN_REFS:])
    ctx, seq = norms.ctx, norms.seq
    length = q_ref.shape[0]
    scale = 1.0 / math.sqrt(QK_DIM)

    barrier = pltpu.get_barrier_semaphore()
    for i in range(1, n_ctx):
        pl.semaphore_signal(
            barrier, inc=1, device_id=(lax.rem(ctx + i, n_ctx), seq), device_id_type=MESH
        )
    for i in range(1, n_seq):
        pl.semaphore_signal(
            barrier, inc=1, device_id=(ctx, lax.rem(seq + i, n_seq)), device_id_type=MESH
        )

    def wide(head):
        return pl.ds(pl.multiple_of(head * HEAD_DIM, HEAD_DIM), HEAD_DIM)

    def narrow(head):
        return pl.ds(pl.multiple_of(head * QK_DIM, QK_DIM), QK_DIM)

    def one(head):
        return pl.ds(head, 1)

    def indicator():
        return jnp.where(
            iota((HEADS, LANES), 1) // QK_DIM == iota((HEADS, LANES), 0), 1.0, 0.0
        ).astype(BF16)

    def causal():
        return iota((length, length), 0) <= iota((length, length), 1)

    def scores(head):
        return dot(kt16[narrow(head), :], qt16[narrow(head), :], TN)

    def kernel_of(s):
        return jnp.where(causal(), 1.0 + s + 0.5 * s * s, 0.0)

    def arrives(n, source, target):
        return pltpu.make_async_copy(source, target, load_sem.at[n])

    loads = [arrives(0, k_in, k_ref), arrives(1, v_in, v_ref), arrives(2, q_in, q_ref), arrives(3, g_in, g_ref)]
    for load in loads:
        load.start()
    loads[0].wait()
    kt[...] = k_ref[...].astype(F32).T
    kt16[...] = kt[...].astype(BF16)
    norms.own[0:QK_DIM, :] = compact(dot(k_ref[...], k_ref[...], TN))
    norms.own[QK_DIM:, :] = dot(jnp.ones((8, length), BF16), k_ref[...])

    def key_state(scan, head, carry):
        high, low = split(features(kt[narrow(head), :]))
        phik[head, 0:ROWS, :] = high
        phik[head, ROWS : 2 * ROWS, :] = low
        phik[head, 2 * ROWS : 3 * ROWS, :] = high
        scan.put(head, dot2((high, low), v_ref[:, wide(head)]))
        return carry

    def prepare(head, carry):
        kern = kernel_of(scores(head))
        den[one(head), :] = jnp.sum(kern, axis=0, keepdims=True)
        numer[head] = dot2r(v_ref[:, wide(head)], split(kern), TN)
        return carry

    def begin(scan, head, carry):
        scan.begin(head)
        return carry

    loads[1].wait()
    for scan, _, _ in earlier:
        lax.fori_loop(scan.first, scan.first + scan.count, functools.partial(key_state, scan), 0)
    pl.semaphore_wait(barrier, n_ctx + n_seq - 2)
    norms.start()
    for scan, _, _ in earlier:
        lax.fori_loop(scan.first, scan.first + scan.count, functools.partial(begin, scan), 0)
    loads[2].wait()
    qt[...] = q_ref[...].astype(F32).T
    qt16[...] = (qt[...] * scale).astype(BF16)
    loads[3].wait()
    lax.fori_loop(0, HEADS, prepare, 0)

    def norm_turn(_):
        norms.turn()

    def norm_done(_):
        prior = norms.result()
        square = split(blocks(prior[:QK_DIM]))
        linear = prior[QK_DIM : QK_DIM + 1, :] * scale
        y = dot2r(q_ref[...], square)
        yn[...] = y * (scale * scale) + linear
        z = q_ref[...].astype(F32) * (y * (0.5 * scale * scale) + linear)
        count = (length * (seq * n_ctx + ctx)).astype(F32)
        rden[...] = 1.0 / (den[...] + dot2r(indicator(), split(z), NT) + count)

    def query_state(scan, head):
        phi = features(qt[narrow(head), :])
        high, low = split(phi)
        phiq[head, 0:ROWS, :] = high
        phiq[head, ROWS : 2 * ROWS, :] = low
        phiq[head, 2 * ROWS : 3 * ROWS, :] = high
        scan.put(head, dot2(split(phi * rden[one(head), :]), g_ref[:, wide(head)]))
        scan.begin(head)

    def local_values(head):
        kern = kernel_of(scores(head)) * rden[one(head), :]
        gv_acc[head] = dot2(split(kern), g_ref[:, wide(head)])

    def middle(scan, head):
        g = g_ref[:, wide(head)]
        high, low = split(weighed(scan.result(head)))
        row = rden[one(head), :]
        state = jnp.concatenate([high, high, low], axis=0)
        out = (numer[head] + dot(state, phiq[head], TN)) * row
        out_ref[:, wide(head)] = out.T.astype(BF16)
        share = jnp.sum(g.astype(F32).T * out, axis=0, keepdims=True) * row
        shares[one(head), :] = share
        grad = dot(jnp.concatenate([high, low], axis=1), jnp.concatenate([g, g], axis=1), NT)
        gqt[narrow(head), :] = pull(grad, qt[narrow(head), :]) * row

    def local_gradients(head):
        s = scores(head)
        direct = dot(v_ref[:, wide(head)], g_ref[:, wide(head)], NT)
        direct = direct * rden[one(head), :] - shares[one(head), :]
        grad = split(jnp.where(causal(), direct * (1.0 + s), 0.0))
        gqt[narrow(head), :] += dot2r(kt16[narrow(head), :], grad) * scale
        gkt[narrow(head), :] = dot2r(qt16[narrow(head), :], grad, NT)

    def share_start(_):
        spread = dot2(split(shares[...]), indicator(), TN)
        gq_ref[...] = (gqt[...].T - spread * yn[...]).astype(BF16)
        part = split(q_ref[...].astype(F32) * spread)
        pulls.own[0:QK_DIM, :] = compact(dot2r(q_ref[...], part, TN))
        pulls.own[QK_DIM:, :] = dot2r(jnp.ones((8, length), BF16), part)
        pulls.start()

    def share_turn(_):
        pulls.turn()

    def last(scan, head):
        v = v_ref[:, wide(head)]
        high, low = split(weighed(scan.result(head)))
        state = jnp.concatenate([high, high, low], axis=0)
        grad_v = gv_acc[head] + dot(phik[head], state, TN)
        gv_ref[:, wide(head)] = grad_v.astype(BF16)
        grad = dot(jnp.concatenate([high, low], axis=1), jnp.concatenate([v, v], axis=1), NT)
        gkt[narrow(head), :] += pull(grad, kt[narrow(head), :])

    def values_too(scan, head):
        query_state(scan, head)
        local_values(head)

    def gradients_too(scan, head):
        middle(scan, head)
        local_gradients(head)

    plan, work, share_at, end = [], [], 0, 0
    for scan, start, lags in earlier:
        stages, done = scan.stages(start, lags)
        plan += stages
        work.append(scan.heads(functools.partial(gradients_too, scan), done))
        share_at = max(share_at, done + (scan.count - 1) * PIECES + 1)
    for scan, start, lags in later:
        stages, done = scan.stages(start, lags)
        plan += stages
        work.append(scan.heads(functools.partial(values_too, scan), start))
        work.append(scan.heads(functools.partial(last, scan), done))
        end = max(end, done + (scan.count - 1) * PIECES + 1)
    end = max(end, share_at + SHARE_LAG + 1)
    plan += [(norm_turn, NORM_TURN, 1, 1, None), (norm_done, NORM_DONE, 1, 1, None)] + work
    plan += [(share_start, share_at, 1, 1, None), (share_turn, share_at + SHARE_LAG, 1, 1, None)]

    def turn(u, carry):
        for half in range(PIECES):
            for body, start, stride, count, condition in plan:
                if isinstance(start, int) and (stride == PIECES or count == 1):
                    if (half - start) % PIECES:
                        continue
                    item = u - (start - half) // PIECES
                else:
                    past = u * PIECES + half - start
                    item = past // stride
                if count == 1:
                    ok = item == 0
                else:
                    ok = (item >= 0) & (item < count)
                if stride > 1 and not isinstance(start, int):
                    ok = ok & (past % stride == 0)

                @pl.when(ok if condition is None else ok & condition)
                def _(body=body, item=item):
                    body(item)

        return carry

    lax.fori_loop(0, (end + PIECES - 1) // PIECES, turn, 0)
    after = pulls.result()
    square = split(blocks(after[:QK_DIM]))
    norm = dot2r(k_ref[...], square) * (scale * scale) + after[QK_DIM : QK_DIM + 1, :] * scale
    gk_ref[...] = (gkt[...].T - norm).astype(BF16)

    for scan, _, _ in earlier + later:
        scan.finish()
    norms.finish()
    pulls.finish()


def deliver(*refs):
    sem = refs[8]
    copies = [pltpu.make_async_copy(refs[i], refs[4 + i], sem.at[i]) for i in range(4)]
    for copy in copies:
        copy.start()
    for copy in copies:
        copy.wait()


def small_refs(n_ctx, n_seq):
    rows = QK_DIM + 8
    one = pltpu.VMEM((rows, LANES), F32)
    semaphores = pltpu.SemaphoreType.DMA((2,))
    return [
        one, pltpu.VMEM((n_ctx - 1, rows, LANES), F32), one, one,
        pltpu.VMEM((n_seq - 1, rows, LANES), F32), semaphores, semaphores,
    ]


def scan_refs(n_seq):
    rounds = radices(n_seq // 2)
    slots = sum(rounds) - len(rounds)
    full = pltpu.VMEM((HEADS, ROWS, LANES), F32)
    parts = pltpu.VMEM((len(rounds), HEADS, HALF, LANES), F32)
    halves = pltpu.VMEM((slots, HEADS, HALF, LANES), F32)
    send = pltpu.SemaphoreType.DMA((slots + 4,))
    chain = pltpu.SemaphoreType.DMA((2, CHUNKS))
    receive = pltpu.SemaphoreType.DMA((len(rounds) + 2, HEADS))
    return [full, full, full, parts, halves, full, full, full, full, full, send, chain, receive]


def per_device(n_ctx, n_seq, queries, keys, values, grad_output):
    length = queries.shape[0]
    across = pltpu.VMEM((LANES, length), F32)
    across16 = pltpu.VMEM((LANES, length), BF16)
    rows = pltpu.VMEM((HEADS, length), F32)
    stacked = pltpu.VMEM((HEADS, 3 * ROWS, length), BF16)
    narrow, broad = pltpu.VMEM(queries.shape, BF16), pltpu.VMEM(values.shape, BF16)
    scratch = [
        narrow, narrow, broad, broad, pltpu.SemaphoreType.DMA((4,)),
        across, across, across16, across16, rows, rows, rows,
        pltpu.VMEM((length, LANES), F32),
        pltpu.VMEM((HEADS, HEAD_DIM, length), F32),
        pltpu.VMEM((HEADS, length, HEAD_DIM), F32),
        across, across, stacked, stacked,
    ]
    scratch += small_refs(n_ctx, n_seq) * 2 + scan_refs(n_seq) * 2
    anywhere = pl.BlockSpec(memory_space=pl.ANY)
    inside = pl.BlockSpec(memory_space=pltpu.VMEM)
    results = pl.pallas_call(
        functools.partial(kernel, n_ctx, n_seq),
        out_shape=(broad, narrow, narrow, broad),
        in_specs=[anywhere] * 4,
        out_specs=(inside,) * 4,
        scratch_shapes=scratch,
        compiler_params=pltpu.CompilerParams(
            collective_id=0, has_side_effects=True, vmem_limit_bytes=56 << 20
        ),
        name="attention",
    )(queries, keys, values, grad_output)
    return pl.pallas_call(
        deliver,
        out_shape=tuple(jax.ShapeDtypeStruct(a.shape, a.dtype) for a in results),
        in_specs=[inside] * 4,
        out_specs=(anywhere,) * 4,
        scratch_shapes=[pltpu.SemaphoreType.DMA((4,))],
        name="deliver",
    )(*(pltpu.with_memory_space_constraint(a, pltpu.VMEM) for a in results))


def solution(mesh):
    placed = P(("seq", "ctx"), None)
    return jax.shard_map(
        functools.partial(per_device, mesh.shape["ctx"], mesh.shape["seq"]),
        mesh=mesh,
        in_specs=(placed,) * 4,
        out_specs=(placed,) * 4,
        check_vma=False,
    )
```

```python
import functools
import math

import jax
import jax.numpy as jnp
from jax import lax
from jax.experimental import pallas as pl
from jax.experimental.pallas import tpu as pltpu
from jax.sharding import PartitionSpec as P

HEADS = 8
QK_DIM = 16
HEAD_DIM = 128
LANES = 128
ROWS = 160
HALF = ROWS // 2
PIECES = 2
CHUNKS = HEADS * PIECES
PIECE = ROWS // PIECES
MESH = pl.DeviceIdType.MESH
NN = (((1,), (0,)), ((), ()))
NT = (((1,), (1,)), ((), ()))
TN = (((0,), (0,)), ((), ()))
F32 = jnp.float32
BF16 = jnp.bfloat16


def dot(a, b, dims=NN):
    return lax.dot_general(a, b, dims, preferred_element_type=F32)


def split(x):
    high = x.astype(BF16)
    return high, (x - high.astype(F32)).astype(BF16)


def dot2(pair, b, dims=NN):
    return dot(pair[0], b, dims) + dot(pair[1], b, dims)


def dot2r(a, pair, dims=NN):
    return dot(a, pair[0], dims) + dot(a, pair[1], dims)


def iota(shape, dim):
    return lax.broadcasted_iota(jnp.int32, shape, dim)


def shifted(x, d):
    return pltpu.roll(x, d % QK_DIM, 0)


def features(x):
    half = QK_DIM // 2
    parts = [x, x * x]
    for d in range(1, half):
        parts.append(x * shifted(x, -d))
    parts.append(x[:half] * x[half:])
    parts.append(jnp.where(iota((8, x.shape[1]), 0) == 0, 1.0, 0.0))
    return jnp.concatenate(parts, axis=0)


def weighed(state):
    w = QK_DIM
    last = ROWS - 8
    return jnp.concatenate(
        [
            state[:w] * (1.0 / math.sqrt(w)),
            state[w : 2 * w] * (0.5 / w),
            state[2 * w : last] * (1.0 / w),
            state[last:],
        ],
        axis=0,
    )


def pull(grad, x):
    w, half = QK_DIM, QK_DIM // 2
    total = grad[:w] + 2.0 * grad[w : 2 * w] * x
    for d in range(1, half):
        rows = grad[w * (d + 1) : w * (d + 2)]
        total = total + rows * shifted(x, -d) + shifted(rows * x, d)
    rows = grad[w * (half + 1) : w * (half + 1) + half]
    return total + jnp.concatenate([rows * x[half:], rows * x[:half]], axis=0)


def own_block():
    return iota((LANES, LANES), 0) // QK_DIM == iota((LANES, LANES), 1) // QK_DIM


def compact(square):
    kept = jnp.where(own_block(), square, 0.0)
    total = kept[:QK_DIM]
    for h in range(1, HEADS):
        total = total + kept[h * QK_DIM : (h + 1) * QK_DIM]
    return total


def blocks(rows):
    return jnp.where(own_block(), jnp.concatenate([rows] * HEADS, axis=0), 0.0)


class Small:
    def __init__(self, n_ctx, n_seq, reverse, refs):
        self.own, self.got, self.total, self.kept, self.far, self.send_sem, self.recv_sem = refs
        self.n_ctx, self.n_seq, self.reverse = n_ctx, n_seq, reverse
        self.ctx, self.seq = lax.axis_index("ctx"), lax.axis_index("seq")

    def copy(self, source, target, n, device):
        return pltpu.make_async_remote_copy(
            src_ref=source,
            dst_ref=target,
            send_sem=self.send_sem.at[n],
            recv_sem=self.recv_sem.at[n],
            device_id=device,
            device_id_type=MESH,
        )

    def near_to(self, i):
        return (lax.rem(self.ctx + i, self.n_ctx), self.seq)

    def far_to(self, i):
        return (self.ctx, lax.rem(self.seq + i, self.n_seq))

    def near_all(self):
        return self.copy(self.got, self.got, 0, self.near_to(1))

    def far_all(self):
        return self.copy(self.far, self.far, 1, self.far_to(1))

    def before(self, place, i):
        return place < i if self.reverse else place >= i

    def start(self):
        for i in range(1, self.n_ctx):
            self.copy(self.own, self.got.at[i - 1], 0, self.near_to(i)).start()

    def turn(self):
        total = self.own[...]
        kept = jnp.zeros_like(total)
        self.near_all().wait_recv()
        for i in range(1, self.n_ctx):
            arrived = self.got[i - 1]
            total = total + arrived
            kept = kept + jnp.where(self.before(self.ctx, i), arrived, 0.0)
        self.total[...] = total
        self.kept[...] = kept
        for i in range(1, self.n_seq):
            self.copy(self.total, self.far.at[i - 1], 1, self.far_to(i)).start()

    def result(self):
        kept = self.kept[...]
        self.far_all().wait_recv()
        for i in range(1, self.n_seq):
            kept = kept + jnp.where(self.before(self.seq, i), self.far[i - 1], 0.0)
        return kept

    def finish(self):
        self.near_all().wait_send()
        self.far_all().wait_send()


def radices(pairs):
    out = []
    while pairs > 1:
        out.append(4 if pairs % 4 == 0 else 2)
        pairs //= out[-1]
    return out


class Scan:
    def __init__(self, n_ctx, n_seq, reverse, first, count, refs):
        self.first, self.count = first, count
        (
            self.x, self.total, self.peer, self.part, self.got, self.before,
            self.up, self.up_got, self.down, self.down_got, self.send_sem, self.chain_sem, self.recv_sem,
        ) = refs
        ctx, seq = lax.axis_index("ctx"), lax.axis_index("seq")
        step = -1 if reverse else 1
        self.step, self.ctx, self.seq = step, ctx, seq
        self.n_ctx = n_ctx
        self.place = n_ctx - 1 - ctx if reverse else ctx
        line = n_seq - 1 - seq if reverse else seq
        self.mine = line % 2
        self.radices = radices(n_seq // 2)
        self.digits, self.strides, self.slots = [], [], []
        stride = slot = 0
        stride = 1
        for radix in self.radices:
            self.digits.append((line // 2 // stride) % radix)
            self.strides.append(stride)
            self.slots.append(slot)
            stride, slot = stride * radix, slot + radix - 1
        self.n_slots = slot
        self.has_above = self.place < n_ctx - 1
        self.has_below = self.place > 0
        self.above = (lax.rem(ctx + step + n_ctx, n_ctx), seq)
        self.below = (lax.rem(ctx - step + n_ctx, n_ctx), seq)
        self.core = (ctx, seq + step * (1 - 2 * self.mine))

    def rows(self, half):
        return pl.ds(pl.multiple_of(half * HALF, HALF), HALF)

    def piece(self, c):
        return c // PIECES, pl.ds(pl.multiple_of(c % PIECES * PIECE, PIECE), PIECE)

    def copy(self, n, receive, source, target, device):
        return pltpu.make_async_remote_copy(
            src_ref=source,
            dst_ref=target,
            send_sem=self.send_sem.at[n],
            recv_sem=receive,
            device_id=device,
            device_id_type=MESH,
        )

    def upward(self, c):
        at = self.piece(c)
        return self.copy(0, self.chain_sem.at[0, c], self.up.at[at], self.up_got.at[at], self.above)

    def downward(self, c):
        at = self.piece(c)
        return self.copy(
            1, self.chain_sem.at[1, c], self.down.at[at], self.down_got.at[at], self.below
        )

    def swap(self, c):
        return self.copy(2, self.recv_sem.at[0, c], self.total.at[c], self.peer.at[c], self.core)

    def share(self, c):
        half = self.before.at[c, self.rows(self.mine)]
        return self.copy(3, self.recv_sem.at[1, c], half, half, self.core)

    def exchange(self, r, i, c):
        radix, digit, stride = self.radices[r], self.digits[r], self.strides[r]
        move = (lax.rem(digit + i, radix) - digit) * stride * 2
        slot = self.slots[r] + i - 1
        return self.copy(
            4 + slot, self.recv_sem.at[2 + r, c], self.part.at[r, c], self.got.at[slot, c],
            (self.ctx, self.seq + self.step * move),
        )

    def arrive(self, r, c):
        def wait(n):
            slots = self.got.at[self.slots[r] : self.slots[r] + n, c]
            self.copy(4, self.recv_sem.at[2 + r, c], slots, slots, self.core).wait_recv()

        radix = self.radices[r]
        if r < len(self.radices) - 1:
            wait(radix - 1)
        else:
            for n in range(1, radix):
                pl.when(self.digits[r] == n)(functools.partial(wait, n))

    def sends(self, r, i):
        return self.digits[r] + i < self.radices[r] if r == len(self.radices) - 1 else None

    def guarded(self, condition, action):
        if condition is None:
            action()
        else:
            pl.when(condition)(action)

    def send_part(self, r, c):
        for i in range(1, self.radices[r]):
            self.guarded(self.sends(r, i), lambda i=i: self.exchange(r, i, c).start())

    def pair(self, c):
        self.swap(c).wait_recv()
        half = self.rows(self.mine)
        self.part[0, c] = self.total[c, half] + self.peer[c, half]
        self.send_part(0, c)

    def round(self, r, c):
        last = r == len(self.radices) - 1
        kept = jnp.zeros((HALF, LANES), F32)
        if r:
            kept = self.before[c, self.rows(self.mine)]
        total = None if last else self.part[r, c]
        self.arrive(r, c)
        for i in range(1, self.radices[r]):
            arrived = self.got[self.slots[r] + i - 1, c]
            kept = kept + jnp.where(self.digits[r] >= i, arrived, 0.0)
            if not last:
                total = total + arrived
        self.before[c, self.rows(self.mine)] = kept
        if last:
            self.share(c).start()
        else:
            self.part[r + 1, c] = total
            self.send_part(r + 1, c)

    def outer(self, c):
        return self.before[c] + jnp.where(self.mine == 1, self.peer[c], 0.0)

    def sent(self, n, source, target):
        self.copy(n, self.recv_sem.at[0, 0], source, target, self.core).wait_send()

    def finish(self):
        mine = pl.ds(self.first, self.count)
        self.sent(2, self.total.at[mine], self.peer.at[mine])
        half = self.before.at[mine, self.rows(self.mine)]
        self.sent(3, half, half)
        for r in range(len(self.radices)):
            for i in range(1, self.radices[r]):
                slot = self.slots[r] + i - 1
                part, got = self.part.at[r, mine], self.got.at[slot, mine]
                self.guarded(
                    self.sends(r, i),
                    lambda slot=slot, part=part, got=got: self.sent(4 + slot, part, got),
                )

        @pl.when(self.has_below)
        def _():
            self.sent(1, self.down.at[mine], self.down_got.at[mine])

        @pl.when(self.has_above)
        def _():
            self.sent(0, self.up.at[mine], self.up_got.at[mine])

    def heads(self, body, start):
        return lambda i: body(i + self.first), start, PIECES, self.count, None

    def chunks(self, body, start, condition):
        return lambda i: body(i + self.first * PIECES), start, 1, self.count * PIECES, condition

    def outer_stages(self, at, lags):
        pair_lag, round_lag, share_lag, _ = lags
        at += pair_lag
        out = [self.heads(self.pair, at)]
        for r in range(len(self.radices)):
            at += round_lag
            out.append(self.heads(functools.partial(self.round, r), at))
        at += share_lag
        out.append(self.heads(self.joined, at))
        return out, at

    def inner_stages(self, at, lags):
        hop_lag, n = lags[3], self.n_ctx - 1
        return [
            self.chunks(self.rise, at + hop_lag * self.place, self.has_below),
            self.chunks(self.sink, at + hop_lag * (n - self.place), self.has_above),
        ]


class Inner(Scan):
    def put(self, head, state):
        self.x[head] = state
        self.up[head] = state
        self.down[head] = state

    def begin(self, head):
        for p in range(PIECES):
            c = head * PIECES + p

            @pl.when(self.has_above & ~self.has_below)
            def _(c=c):
                self.upward(c).start()

            @pl.when(self.has_below & ~self.has_above)
            def _(c=c):
                self.downward(c).start()

    def rise(self, c):
        self.upward(c).wait_recv()

        @pl.when(self.has_above)
        def _():
            at = self.piece(c)
            self.up[at] = self.x[at] + self.up_got[at]
            self.upward(c).start()

    def sink(self, c):
        self.downward(c).wait_recv()

        @pl.when(self.has_below)
        def _():
            at = self.piece(c)
            self.down[at] = self.x[at] + self.down_got[at]
            self.downward(c).start()

    def whole(self, c):
        total = self.x[c] + jnp.where(self.has_below, self.up_got[c], 0.0)
        self.total[c] = total + jnp.where(self.has_above, self.down_got[c], 0.0)
        self.swap(c).start()

    def joined(self, c):
        self.share(c).wait_recv()

    def result(self, c):
        return self.outer(c) + jnp.where(self.has_below, self.up_got[c], 0.0)

    def stages(self, start, lags):
        n = self.n_ctx - 1
        chain = self.inner_stages(start, lags)
        start += PIECES - 1
        whole = self.heads(self.whole, start + lags[3] * jnp.maximum(self.place, n - self.place))
        out, done = self.outer_stages(start + lags[3] * n, lags)
        return chain + [whole] + out, done


class Outer(Scan):
    def put(self, head, state):
        self.total[head] = state

    def begin(self, head):
        self.swap(head).start()

    def joined(self, c):
        self.share(c).wait_recv()

        @pl.when(self.has_above & ~self.has_below)
        def _():
            self.up[c] = self.outer(c) + self.total[c]
            for p in range(PIECES):
                self.upward(c * PIECES + p).start()

        @pl.when(self.has_below & ~self.has_above)
        def _():
            self.down[c] = self.outer(c)
            for p in range(PIECES):
                self.downward(c * PIECES + p).start()

    def rise(self, c):
        self.upward(c).wait_recv()

        @pl.when(self.has_above)
        def _():
            at = self.piece(c)
            self.up[at] = self.outer(at) + self.total[at] + self.up_got[at]
            self.upward(c).start()

    def sink(self, c):
        self.downward(c).wait_recv()

        @pl.when(self.has_below)
        def _():
            at = self.piece(c)
            self.down[at] = self.outer(at) + self.down_got[at]
            self.downward(c).start()

    def result(self, c):
        total = self.outer(c) + jnp.where(self.has_below, self.up_got[c], 0.0)
        return total + jnp.where(self.has_above, self.down_got[c], 0.0)

    def stages(self, start, lags):
        out, at = self.outer_stages(start, lags)
        return out + self.inner_stages(at, lags), at + lags[3] * (self.n_ctx - 1) + PIECES - 1


SMALL_REFS = 7
SCAN_REFS = 13
EARLY = ((Inner, 6, -5, (1, 5, 2, 5)), (Outer, 2, 0, (1, 4, 1, 5)),)
LATE = ((Inner, 3, 10, (1, 7, 2, 5)), (Outer, 5, 7, (2, 6, 2, 5)),)
NORM_TURN = 0
NORM_DONE = 5
SHARE_LAG = 5


def kernel(
    n_ctx, n_seq, q_in, k_in, v_in, g_in, out_ref, gq_ref, gk_ref, gv_ref,
    q_ref, k_ref, v_ref, g_ref, load_sem, qt, kt, qt16, kt16, den, rden, shares, yn, numer, gv_acc, gqt, gkt, phik, phiq, *refs,
):
    norms = Small(n_ctx, n_seq, False, refs[:SMALL_REFS])
    pulls = Small(n_ctx, n_seq, True, refs[SMALL_REFS : 2 * SMALL_REFS])
    refs = refs[2 * SMALL_REFS :]

    def groups(table, reverse, refs):
        out, first = [], 0
        for kind, count, start, lags in table:
            out.append((kind(n_ctx, n_seq, reverse, first, count, refs), start, lags))
            first += count
        return out

    earlier = groups(EARLY, False, refs[:SCAN_REFS])
    later = groups(LATE, True, refs[SCAN_REFS:])
    ctx, seq = norms.ctx, norms.seq
    length = q_ref.shape[0]
    scale = 1.0 / math.sqrt(QK_DIM)

    barrier = pltpu.get_barrier_semaphore()
    for i in range(1, n_ctx):
        pl.semaphore_signal(
            barrier, inc=1, device_id=(lax.rem(ctx + i, n_ctx), seq), device_id_type=MESH
        )
    for i in range(1, n_seq):
        pl.semaphore_signal(
            barrier, inc=1, device_id=(ctx, lax.rem(seq + i, n_seq)), device_id_type=MESH
        )

    def wide(head):
        return pl.ds(pl.multiple_of(head * HEAD_DIM, HEAD_DIM), HEAD_DIM)

    def narrow(head):
        return pl.ds(pl.multiple_of(head * QK_DIM, QK_DIM), QK_DIM)

    def one(head):
        return pl.ds(head, 1)

    def indicator():
        return jnp.where(
            iota((HEADS, LANES), 1) // QK_DIM == iota((HEADS, LANES), 0), 1.0, 0.0
        ).astype(BF16)

    def causal():
        return iota((length, length), 0) <= iota((length, length), 1)

    def scores(head):
        return dot(kt16[narrow(head), :], qt16[narrow(head), :], TN)

    def kernel_of(s):
        return jnp.where(causal(), 1.0 + s + 0.5 * s * s, 0.0)

    def arrives(n, source, target):
        return pltpu.make_async_copy(source, target, load_sem.at[n])

    loads = [arrives(0, k_in, k_ref), arrives(1, v_in, v_ref), arrives(2, q_in, q_ref), arrives(3, g_in, g_ref)]
    for load in loads:
        load.start()
    loads[0].wait()
    kt[...] = k_ref[...].astype(F32).T
    kt16[...] = kt[...].astype(BF16)
    norms.own[0:QK_DIM, :] = compact(dot(k_ref[...], k_ref[...], TN))
    norms.own[QK_DIM:, :] = dot(jnp.ones((8, length), BF16), k_ref[...])

    def key_state(scan, head, carry):
        high, low = split(features(kt[narrow(head), :]))
        phik[head, 0:ROWS, :] = high
        phik[head, ROWS : 2 * ROWS, :] = low
        phik[head, 2 * ROWS : 3 * ROWS, :] = high
        scan.put(head, dot2((high, low), v_ref[:, wide(head)]))
        return carry

    def prepare(head, carry):
        kern = kernel_of(scores(head))
        den[one(head), :] = jnp.sum(kern, axis=0, keepdims=True)
        numer[head] = dot2r(v_ref[:, wide(head)], split(kern), TN)
        return carry

    def begin(scan, head, carry):
        scan.begin(head)
        return carry

    loads[1].wait()
    for scan, _, _ in earlier:
        lax.fori_loop(scan.first, scan.first + scan.count, functools.partial(key_state, scan), 0)
    pl.semaphore_wait(barrier, n_ctx + n_seq - 2)
    norms.start()
    for scan, _, _ in earlier:
        lax.fori_loop(scan.first, scan.first + scan.count, functools.partial(begin, scan), 0)
    loads[2].wait()
    qt[...] = q_ref[...].astype(F32).T
    qt16[...] = (qt[...] * scale).astype(BF16)
    loads[3].wait()
    lax.fori_loop(0, HEADS, prepare, 0)

    def norm_turn(_):
        norms.turn()

    def norm_done(_):
        prior = norms.result()
        square = split(blocks(prior[:QK_DIM]))
        linear = prior[QK_DIM : QK_DIM + 1, :] * scale
        y = dot2r(q_ref[...], square)
        yn[...] = y * (scale * scale) + linear
        z = q_ref[...].astype(F32) * (y * (0.5 * scale * scale) + linear)
        count = (length * (seq * n_ctx + ctx)).astype(F32)
        rden[...] = 1.0 / (den[...] + dot2r(indicator(), split(z), NT) + count)

    def query_state(scan, head):
        phi = features(qt[narrow(head), :])
        high, low = split(phi)
        phiq[head, 0:ROWS, :] = high
        phiq[head, ROWS : 2 * ROWS, :] = low
        phiq[head, 2 * ROWS : 3 * ROWS, :] = high
        scan.put(head, dot2(split(phi * rden[one(head), :]), g_ref[:, wide(head)]))
        scan.begin(head)

    def local_values(head):
        kern = kernel_of(scores(head)) * rden[one(head), :]
        gv_acc[head] = dot2(split(kern), g_ref[:, wide(head)])

    def middle(scan, head):
        g = g_ref[:, wide(head)]
        high, low = split(weighed(scan.result(head)))
        row = rden[one(head), :]
        state = jnp.concatenate([high, high, low], axis=0)
        out = (numer[head] + dot(state, phiq[head], TN)) * row
        out_ref[:, wide(head)] = out.T.astype(BF16)
        share = jnp.sum(g.astype(F32).T * out, axis=0, keepdims=True) * row
        shares[one(head), :] = share
        grad = dot(jnp.concatenate([high, low], axis=1), jnp.concatenate([g, g], axis=1), NT)
        gqt[narrow(head), :] = pull(grad, qt[narrow(head), :]) * row

    def local_gradients(head):
        s = scores(head)
        direct = dot(v_ref[:, wide(head)], g_ref[:, wide(head)], NT)
        direct = direct * rden[one(head), :] - shares[one(head), :]
        grad = split(jnp.where(causal(), direct * (1.0 + s), 0.0))
        gqt[narrow(head), :] += dot2r(kt16[narrow(head), :], grad) * scale
        gkt[narrow(head), :] = dot2r(qt16[narrow(head), :], grad, NT)

    def share_start(_):
        spread = dot2(split(shares[...]), indicator(), TN)
        gq_ref[...] = (gqt[...].T - spread * yn[...]).astype(BF16)
        part = split(q_ref[...].astype(F32) * spread)
        pulls.own[0:QK_DIM, :] = compact(dot2r(q_ref[...], part, TN))
        pulls.own[QK_DIM:, :] = dot2r(jnp.ones((8, length), BF16), part)
        pulls.start()

    def share_turn(_):
        pulls.turn()

    def last(scan, head):
        v = v_ref[:, wide(head)]
        high, low = split(weighed(scan.result(head)))
        state = jnp.concatenate([high, high, low], axis=0)
        grad_v = gv_acc[head] + dot(phik[head], state, TN)
        gv_ref[:, wide(head)] = grad_v.astype(BF16)
        grad = dot(jnp.concatenate([high, low], axis=1), jnp.concatenate([v, v], axis=1), NT)
        gkt[narrow(head), :] += pull(grad, kt[narrow(head), :])

    def values_too(scan, head):
        query_state(scan, head)
        local_values(head)

    def gradients_too(scan, head):
        middle(scan, head)
        local_gradients(head)

    plan, work, share_at, end = [], [], 0, 0
    for scan, start, lags in earlier:
        stages, done = scan.stages(start, lags)
        plan += stages
        work.append(scan.heads(functools.partial(gradients_too, scan), done))
        share_at = max(share_at, done + (scan.count - 1) * PIECES + 1)
    for scan, start, lags in later:
        stages, done = scan.stages(start, lags)
        plan += stages
        work.append(scan.heads(functools.partial(values_too, scan), start))
        work.append(scan.heads(functools.partial(last, scan), done))
        end = max(end, done + (scan.count - 1) * PIECES + 1)
    end = max(end, share_at + SHARE_LAG + 1)
    plan += [(norm_turn, NORM_TURN, 1, 1, None), (norm_done, NORM_DONE, 1, 1, None)] + work
    plan += [(share_start, share_at, 1, 1, None), (share_turn, share_at + SHARE_LAG, 1, 1, None)]

    def turn(u, carry):
        for half in range(PIECES):
            for body, start, stride, count, condition in plan:
                if isinstance(start, int) and (stride == PIECES or count == 1):
                    if (half - start) % PIECES:
                        continue
                    item = u - (start - half) // PIECES
                else:
                    past = u * PIECES + half - start
                    item = past // stride
                if count == 1:
                    ok = item == 0
                else:
                    ok = (item >= 0) & (item < count)
                if stride > 1 and not isinstance(start, int):
                    ok = ok & (past % stride == 0)

                @pl.when(ok if condition is None else ok & condition)
                def _(body=body, item=item):
                    body(item)

        return carry

    lax.fori_loop(0, (end + PIECES - 1) // PIECES, turn, 0)
    after = pulls.result()
    square = split(blocks(after[:QK_DIM]))
    norm = dot2r(k_ref[...], square) * (scale * scale) + after[QK_DIM : QK_DIM + 1, :] * scale
    gk_ref[...] = (gkt[...].T - norm).astype(BF16)

    for scan, _, _ in earlier + later:
        scan.finish()
    norms.finish()
    pulls.finish()


def deliver(*refs):
    sem = refs[8]
    copies = [pltpu.make_async_copy(refs[i], refs[4 + i], sem.at[i]) for i in range(4)]
    for copy in copies:
        copy.start()
    for copy in copies:
        copy.wait()


def small_refs(n_ctx, n_seq):
    rows = QK_DIM + 8
    one = pltpu.VMEM((rows, LANES), F32)
    semaphores = pltpu.SemaphoreType.DMA((2,))
    return [
        one, pltpu.VMEM((n_ctx - 1, rows, LANES), F32), one, one,
        pltpu.VMEM((n_seq - 1, rows, LANES), F32), semaphores, semaphores,
    ]


def scan_refs(n_seq):
    rounds = radices(n_seq // 2)
    slots = sum(rounds) - len(rounds)
    full = pltpu.VMEM((HEADS, ROWS, LANES), F32)
    parts = pltpu.VMEM((len(rounds), HEADS, HALF, LANES), F32)
    halves = pltpu.VMEM((slots, HEADS, HALF, LANES), F32)
    send = pltpu.SemaphoreType.DMA((slots + 4,))
    chain = pltpu.SemaphoreType.DMA((2, CHUNKS))
    receive = pltpu.SemaphoreType.DMA((len(rounds) + 2, HEADS))
    return [full, full, full, parts, halves, full, full, full, full, full, send, chain, receive]


def per_device(n_ctx, n_seq, queries, keys, values, grad_output):
    length = queries.shape[0]
    across = pltpu.VMEM((LANES, length), F32)
    across16 = pltpu.VMEM((LANES, length), BF16)
    rows = pltpu.VMEM((HEADS, length), F32)
    stacked = pltpu.VMEM((HEADS, 3 * ROWS, length), BF16)
    narrow, broad = pltpu.VMEM(queries.shape, BF16), pltpu.VMEM(values.shape, BF16)
    scratch = [
        narrow, narrow, broad, broad, pltpu.SemaphoreType.DMA((4,)),
        across, across, across16, across16, rows, rows, rows,
        pltpu.VMEM((length, LANES), F32),
        pltpu.VMEM((HEADS, HEAD_DIM, length), F32),
        pltpu.VMEM((HEADS, length, HEAD_DIM), F32),
        across, across, stacked, stacked,
    ]
    scratch += small_refs(n_ctx, n_seq) * 2 + scan_refs(n_seq) * 2
    anywhere = pl.BlockSpec(memory_space=pl.ANY)
    inside = pl.BlockSpec(memory_space=pltpu.VMEM)
    results = pl.pallas_call(
        functools.partial(kernel, n_ctx, n_seq),
        out_shape=(broad, narrow, narrow, broad),
        in_specs=[anywhere] * 4,
        out_specs=(inside,) * 4,
        scratch_shapes=scratch,
        compiler_params=pltpu.CompilerParams(
            collective_id=0, has_side_effects=True, vmem_limit_bytes=56 << 20
        ),
        name="attention",
    )(queries, keys, values, grad_output)
    return pl.pallas_call(
        deliver,
        out_shape=tuple(jax.ShapeDtypeStruct(a.shape, a.dtype) for a in results),
        in_specs=[inside] * 4,
        out_specs=(anywhere,) * 4,
        scratch_shapes=[pltpu.SemaphoreType.DMA((4,))],
        name="deliver",
    )(*(pltpu.with_memory_space_constraint(a, pltpu.VMEM) for a in results))


def solution(mesh):
    placed = P(("seq", "ctx"), None)
    return jax.shard_map(
        functools.partial(per_device, mesh.shape["ctx"], mesh.shape["seq"]),
        mesh=mesh,
        in_specs=(placed,) * 4,
        out_specs=(placed,) * 4,
        check_vma=False,
    )
```

```python
import functools
import math

import jax
import jax.numpy as jnp
from jax import lax
from jax.experimental import pallas as pl
from jax.experimental.pallas import tpu as pltpu
from jax.sharding import PartitionSpec as P

HEADS = 8
QK_DIM = 16
HEAD_DIM = 128
LANES = 128
ROWS = 160
HALF = ROWS // 2
PIECES = 2
CHUNKS = HEADS * PIECES
PIECE = ROWS // PIECES
MESH = pl.DeviceIdType.MESH
NN = (((1,), (0,)), ((), ()))
NT = (((1,), (1,)), ((), ()))
TN = (((0,), (0,)), ((), ()))
F32 = jnp.float32
BF16 = jnp.bfloat16


def dot(a, b, dims=NN):
    return lax.dot_general(a, b, dims, preferred_element_type=F32)


def split(x):
    high = x.astype(BF16)
    return high, (x - high.astype(F32)).astype(BF16)


def dot2(pair, b, dims=NN):
    return dot(pair[0], b, dims) + dot(pair[1], b, dims)


def dot2r(a, pair, dims=NN):
    return dot(a, pair[0], dims) + dot(a, pair[1], dims)


def iota(shape, dim):
    return lax.broadcasted_iota(jnp.int32, shape, dim)


def shifted(x, d):
    return pltpu.roll(x, d % QK_DIM, 0)


def features(x):
    half = QK_DIM // 2
    parts = [x, x * x]
    for d in range(1, half):
        parts.append(x * shifted(x, -d))
    parts.append(x[:half] * x[half:])
    parts.append(jnp.where(iota((8, x.shape[1]), 0) == 0, 1.0, 0.0))
    return jnp.concatenate(parts, axis=0)


def weighed(state):
    w = QK_DIM
    last = ROWS - 8
    return jnp.concatenate(
        [
            state[:w] * (1.0 / math.sqrt(w)),
            state[w : 2 * w] * (0.5 / w),
            state[2 * w : last] * (1.0 / w),
            state[last:],
        ],
        axis=0,
    )


def pull(grad, x):
    w, half = QK_DIM, QK_DIM // 2
    total = grad[:w] + 2.0 * grad[w : 2 * w] * x
    for d in range(1, half):
        rows = grad[w * (d + 1) : w * (d + 2)]
        total = total + rows * shifted(x, -d) + shifted(rows * x, d)
    rows = grad[w * (half + 1) : w * (half + 1) + half]
    return total + jnp.concatenate([rows * x[half:], rows * x[:half]], axis=0)


def own_block():
    return iota((LANES, LANES), 0) // QK_DIM == iota((LANES, LANES), 1) // QK_DIM


def compact(square):
    kept = jnp.where(own_block(), square, 0.0)
    total = kept[:QK_DIM]
    for h in range(1, HEADS):
        total = total + kept[h * QK_DIM : (h + 1) * QK_DIM]
    return total


def blocks(rows):
    return jnp.where(own_block(), jnp.concatenate([rows] * HEADS, axis=0), 0.0)


class Small:
    def __init__(self, n_ctx, n_seq, reverse, refs):
        self.own, self.got, self.total, self.kept, self.far, self.send_sem, self.recv_sem = refs
        self.n_ctx, self.n_seq, self.reverse = n_ctx, n_seq, reverse
        self.ctx, self.seq = lax.axis_index("ctx"), lax.axis_index("seq")

    def copy(self, source, target, n, device):
        return pltpu.make_async_remote_copy(
            src_ref=source,
            dst_ref=target,
            send_sem=self.send_sem.at[n],
            recv_sem=self.recv_sem.at[n],
            device_id=device,
            device_id_type=MESH,
        )

    def near_to(self, i):
        return (lax.rem(self.ctx + i, self.n_ctx), self.seq)

    def far_to(self, i):
        return (self.ctx, lax.rem(self.seq + i, self.n_seq))

    def near_all(self):
        return self.copy(self.got, self.got, 0, self.near_to(1))

    def far_all(self):
        return self.copy(self.far, self.far, 1, self.far_to(1))

    def before(self, place, i):
        return place < i if self.reverse else place >= i

    def start(self):
        for i in range(1, self.n_ctx):
            self.copy(self.own, self.got.at[i - 1], 0, self.near_to(i)).start()

    def turn(self):
        total = self.own[...]
        kept = jnp.zeros_like(total)
        self.near_all().wait_recv()
        for i in range(1, self.n_ctx):
            arrived = self.got[i - 1]
            total = total + arrived
            kept = kept + jnp.where(self.before(self.ctx, i), arrived, 0.0)
        self.total[...] = total
        self.kept[...] = kept
        for i in range(1, self.n_seq):
            self.copy(self.total, self.far.at[i - 1], 1, self.far_to(i)).start()

    def result(self):
        kept = self.kept[...]
        self.far_all().wait_recv()
        for i in range(1, self.n_seq):
            kept = kept + jnp.where(self.before(self.seq, i), self.far[i - 1], 0.0)
        return kept

    def finish(self):
        self.near_all().wait_send()
        self.far_all().wait_send()


def radices(pairs):
    out = []
    while pairs > 1:
        out.append(4 if pairs % 4 == 0 else 2)
        pairs //= out[-1]
    return out


class Scan:
    def __init__(self, n_ctx, n_seq, reverse, first, count, refs):
        self.first, self.count = first, count
        (
            self.x, self.total, self.peer, self.part, self.got, self.before,
            self.up, self.up_got, self.down, self.down_got, self.send_sem, self.chain_sem, self.recv_sem,
        ) = refs
        ctx, seq = lax.axis_index("ctx"), lax.axis_index("seq")
        step = -1 if reverse else 1
        self.step, self.ctx, self.seq = step, ctx, seq
        self.n_ctx = n_ctx
        self.place = n_ctx - 1 - ctx if reverse else ctx
        line = n_seq - 1 - seq if reverse else seq
        self.mine = line % 2
        self.radices = radices(n_seq // 2)
        self.digits, self.strides, self.slots = [], [], []
        stride = slot = 0
        stride = 1
        for radix in self.radices:
            self.digits.append((line // 2 // stride) % radix)
            self.strides.append(stride)
            self.slots.append(slot)
            stride, slot = stride * radix, slot + radix - 1
        self.n_slots = slot
        self.has_above = self.place < n_ctx - 1
        self.has_below = self.place > 0
        self.above = (lax.rem(ctx + step + n_ctx, n_ctx), seq)
        self.below = (lax.rem(ctx - step + n_ctx, n_ctx), seq)
        self.core = (ctx, seq + step * (1 - 2 * self.mine))

    def rows(self, half):
        return pl.ds(pl.multiple_of(half * HALF, HALF), HALF)

    def piece(self, c):
        return c // PIECES, pl.ds(pl.multiple_of(c % PIECES * PIECE, PIECE), PIECE)

    def copy(self, n, receive, source, target, device):
        return pltpu.make_async_remote_copy(
            src_ref=source,
            dst_ref=target,
            send_sem=self.send_sem.at[n],
            recv_sem=receive,
            device_id=device,
            device_id_type=MESH,
        )

    def upward(self, c):
        at = self.piece(c)
        return self.copy(0, self.chain_sem.at[0, c], self.up.at[at], self.up_got.at[at], self.above)

    def downward(self, c):
        at = self.piece(c)
        return self.copy(
            1, self.chain_sem.at[1, c], self.down.at[at], self.down_got.at[at], self.below
        )

    def swap(self, c):
        return self.copy(2, self.recv_sem.at[0, c], self.total.at[c], self.peer.at[c], self.core)

    def share(self, c):
        half = self.before.at[c, self.rows(self.mine)]
        return self.copy(3, self.recv_sem.at[1, c], half, half, self.core)

    def exchange(self, r, i, c):
        radix, digit, stride = self.radices[r], self.digits[r], self.strides[r]
        move = (lax.rem(digit + i, radix) - digit) * stride * 2
        slot = self.slots[r] + i - 1
        return self.copy(
            4 + slot, self.recv_sem.at[2 + r, c], self.part.at[r, c], self.got.at[slot, c],
            (self.ctx, self.seq + self.step * move),
        )

    def arrive(self, r, c):
        def wait(n):
            slots = self.got.at[self.slots[r] : self.slots[r] + n, c]
            self.copy(4, self.recv_sem.at[2 + r, c], slots, slots, self.core).wait_recv()

        radix = self.radices[r]
        if r < len(self.radices) - 1:
            wait(radix - 1)
        else:
            for n in range(1, radix):
                pl.when(self.digits[r] == n)(functools.partial(wait, n))

    def sends(self, r, i):
        return self.digits[r] + i < self.radices[r] if r == len(self.radices) - 1 else None

    def guarded(self, condition, action):
        if condition is None:
            action()
        else:
            pl.when(condition)(action)

    def send_part(self, r, c):
        for i in range(1, self.radices[r]):
            self.guarded(self.sends(r, i), lambda i=i: self.exchange(r, i, c).start())

    def pair(self, c):
        self.swap(c).wait_recv()
        half = self.rows(self.mine)
        self.part[0, c] = self.total[c, half] + self.peer[c, half]
        self.send_part(0, c)

    def round(self, r, c):
        last = r == len(self.radices) - 1
        kept = jnp.zeros((HALF, LANES), F32)
        if r:
            kept = self.before[c, self.rows(self.mine)]
        total = None if last else self.part[r, c]
        self.arrive(r, c)
        for i in range(1, self.radices[r]):
            arrived = self.got[self.slots[r] + i - 1, c]
            kept = kept + jnp.where(self.digits[r] >= i, arrived, 0.0)
            if not last:
                total = total + arrived
        self.before[c, self.rows(self.mine)] = kept
        if last:
            self.share(c).start()
        else:
            self.part[r + 1, c] = total
            self.send_part(r + 1, c)

    def outer(self, c):
        return self.before[c] + jnp.where(self.mine == 1, self.peer[c], 0.0)

    def sent(self, n, source, target):
        self.copy(n, self.recv_sem.at[0, 0], source, target, self.core).wait_send()

    def finish(self):
        mine = pl.ds(self.first, self.count)
        self.sent(2, self.total.at[mine], self.peer.at[mine])
        half = self.before.at[mine, self.rows(self.mine)]
        self.sent(3, half, half)
        for r in range(len(self.radices)):
            for i in range(1, self.radices[r]):
                slot = self.slots[r] + i - 1
                part, got = self.part.at[r, mine], self.got.at[slot, mine]
                self.guarded(
                    self.sends(r, i),
                    lambda slot=slot, part=part, got=got: self.sent(4 + slot, part, got),
                )

        @pl.when(self.has_below)
        def _():
            self.sent(1, self.down.at[mine], self.down_got.at[mine])

        @pl.when(self.has_above)
        def _():
            self.sent(0, self.up.at[mine], self.up_got.at[mine])

    def heads(self, body, start):
        return lambda i: body(i + self.first), start, PIECES, self.count, None

    def chunks(self, body, start, condition):
        return lambda i: body(i + self.first * PIECES), start, 1, self.count * PIECES, condition

    def outer_stages(self, at, lags):
        pair_lag, round_lag, share_lag, _ = lags
        at += pair_lag
        out = [self.heads(self.pair, at)]
        for r in range(len(self.radices)):
            at += round_lag
            out.append(self.heads(functools.partial(self.round, r), at))
        at += share_lag
        out.append(self.heads(self.joined, at))
        return out, at

    def inner_stages(self, at, lags):
        hop_lag, n = lags[3], self.n_ctx - 1
        return [
            self.chunks(self.rise, at + hop_lag * self.place, self.has_below),
            self.chunks(self.sink, at + hop_lag * (n - self.place), self.has_above),
        ]


class Inner(Scan):
    def put(self, head, state):
        self.x[head] = state
        self.up[head] = state
        self.down[head] = state

    def begin(self, head):
        for p in range(PIECES):
            c = head * PIECES + p

            @pl.when(self.has_above & ~self.has_below)
            def _(c=c):
                self.upward(c).start()

            @pl.when(self.has_below & ~self.has_above)
            def _(c=c):
                self.downward(c).start()

    def rise(self, c):
        self.upward(c).wait_recv()

        @pl.when(self.has_above)
        def _():
            at = self.piece(c)
            self.up[at] = self.x[at] + self.up_got[at]
            self.upward(c).start()

    def sink(self, c):
        self.downward(c).wait_recv()

        @pl.when(self.has_below)
        def _():
            at = self.piece(c)
            self.down[at] = self.x[at] + self.down_got[at]
            self.downward(c).start()

    def whole(self, c):
        total = self.x[c] + jnp.where(self.has_below, self.up_got[c], 0.0)
        self.total[c] = total + jnp.where(self.has_above, self.down_got[c], 0.0)
        self.swap(c).start()

    def joined(self, c):
        self.share(c).wait_recv()

    def result(self, c):
        return self.outer(c) + jnp.where(self.has_below, self.up_got[c], 0.0)

    def stages(self, start, lags):
        n = self.n_ctx - 1
        chain = self.inner_stages(start, lags)
        start += PIECES - 1
        whole = self.heads(self.whole, start + lags[3] * jnp.maximum(self.place, n - self.place))
        out, done = self.outer_stages(start + lags[3] * n, lags)
        return chain + [whole] + out, done


class Outer(Scan):
    def put(self, head, state):
        self.total[head] = state

    def begin(self, head):
        self.swap(head).start()

    def joined(self, c):
        self.share(c).wait_recv()

        @pl.when(self.has_above & ~self.has_below)
        def _():
            self.up[c] = self.outer(c) + self.total[c]
            for p in range(PIECES):
                self.upward(c * PIECES + p).start()

        @pl.when(self.has_below & ~self.has_above)
        def _():
            self.down[c] = self.outer(c)
            for p in range(PIECES):
                self.downward(c * PIECES + p).start()

    def rise(self, c):
        self.upward(c).wait_recv()

        @pl.when(self.has_above)
        def _():
            at = self.piece(c)
            self.up[at] = self.outer(at) + self.total[at] + self.up_got[at]
            self.upward(c).start()

    def sink(self, c):
        self.downward(c).wait_recv()

        @pl.when(self.has_below)
        def _():
            at = self.piece(c)
            self.down[at] = self.outer(at) + self.down_got[at]
            self.downward(c).start()

    def result(self, c):
        total = self.outer(c) + jnp.where(self.has_below, self.up_got[c], 0.0)
        return total + jnp.where(self.has_above, self.down_got[c], 0.0)

    def stages(self, start, lags):
        out, at = self.outer_stages(start, lags)
        return out + self.inner_stages(at, lags), at + lags[3] * (self.n_ctx - 1) + PIECES - 1


SMALL_REFS = 7
SCAN_REFS = 13
EARLY = ((Inner, 6, -5, (1, 5, 2, 5)), (Outer, 2, 0, (1, 4, 1, 5)),)
LATE = ((Inner, 3, 10, (1, 7, 2, 5)), (Outer, 5, 7, (2, 6, 2, 5)),)
NORM_TURN = 0
NORM_DONE = 5
SHARE_LAG = 5


def kernel(
    n_ctx, n_seq, q_in, k_in, v_in, g_in, out_ref, gq_ref, gk_ref, gv_ref,
    q_ref, k_ref, v_ref, g_ref, load_sem, qt, kt, qt16, kt16, den, rden, shares, yn, numer, gv_acc, gqt, gkt, phik, phiq, *refs,
):
    norms = Small(n_ctx, n_seq, False, refs[:SMALL_REFS])
    pulls = Small(n_ctx, n_seq, True, refs[SMALL_REFS : 2 * SMALL_REFS])
    refs = refs[2 * SMALL_REFS :]

    def groups(table, reverse, refs):
        out, first = [], 0
        for kind, count, start, lags in table:
            out.append((kind(n_ctx, n_seq, reverse, first, count, refs), start, lags))
            first += count
        return out

    earlier = groups(EARLY, False, refs[:SCAN_REFS])
    later = groups(LATE, True, refs[SCAN_REFS:])
    ctx, seq = norms.ctx, norms.seq
    length = q_ref.shape[0]
    scale = 1.0 / math.sqrt(QK_DIM)

    barrier = pltpu.get_barrier_semaphore()
    for i in range(1, n_ctx):
        pl.semaphore_signal(
            barrier, inc=1, device_id=(lax.rem(ctx + i, n_ctx), seq), device_id_type=MESH
        )
    for i in range(1, n_seq):
        pl.semaphore_signal(
            barrier, inc=1, device_id=(ctx, lax.rem(seq + i, n_seq)), device_id_type=MESH
        )

    def wide(head):
        return pl.ds(pl.multiple_of(head * HEAD_DIM, HEAD_DIM), HEAD_DIM)

    def narrow(head):
        return pl.ds(pl.multiple_of(head * QK_DIM, QK_DIM), QK_DIM)

    def one(head):
        return pl.ds(head, 1)

    def indicator():
        return jnp.where(
            iota((HEADS, LANES), 1) // QK_DIM == iota((HEADS, LANES), 0), 1.0, 0.0
        ).astype(BF16)

    def causal():
        return iota((length, length), 0) <= iota((length, length), 1)

    def scores(head):
        return dot(kt16[narrow(head), :], qt16[narrow(head), :], TN)

    def kernel_of(s):
        return jnp.where(causal(), 1.0 + s + 0.5 * s * s, 0.0)

    def arrives(n, source, target):
        return pltpu.make_async_copy(source, target, load_sem.at[n])

    loads = [arrives(0, k_in, k_ref), arrives(1, v_in, v_ref), arrives(2, q_in, q_ref), arrives(3, g_in, g_ref)]
    for load in loads:
        load.start()
    loads[0].wait()
    kt[...] = k_ref[...].astype(F32).T
    kt16[...] = kt[...].astype(BF16)
    norms.own[0:QK_DIM, :] = compact(dot(k_ref[...], k_ref[...], TN))
    norms.own[QK_DIM:, :] = dot(jnp.ones((8, length), BF16), k_ref[...])

    def key_state(scan, head, carry):
        high, low = split(features(kt[narrow(head), :]))
        phik[head, 0:ROWS, :] = high
        phik[head, ROWS : 2 * ROWS, :] = low
        phik[head, 2 * ROWS : 3 * ROWS, :] = high
        scan.put(head, dot2((high, low), v_ref[:, wide(head)]))
        return carry

    def prepare(head, carry):
        kern = kernel_of(scores(head))
        den[one(head), :] = jnp.sum(kern, axis=0, keepdims=True)
        numer[head] = dot2r(v_ref[:, wide(head)], split(kern), TN)
        return carry

    def begin(scan, head, carry):
        scan.begin(head)
        return carry

    loads[1].wait()
    for scan, _, _ in earlier:
        lax.fori_loop(scan.first, scan.first + scan.count, functools.partial(key_state, scan), 0)
    pl.semaphore_wait(barrier, n_ctx + n_seq - 2)
    norms.start()
    for scan, _, _ in earlier:
        lax.fori_loop(scan.first, scan.first + scan.count, functools.partial(begin, scan), 0)
    loads[2].wait()
    qt[...] = q_ref[...].astype(F32).T
    qt16[...] = (qt[...] * scale).astype(BF16)
    loads[3].wait()
    lax.fori_loop(0, HEADS, prepare, 0)

    def norm_turn(_):
        norms.turn()

    def norm_done(_):
        prior = norms.result()
        square = split(blocks(prior[:QK_DIM]))
        linear = prior[QK_DIM : QK_DIM + 1, :] * scale
        y = dot2r(q_ref[...], square)
        yn[...] = y * (scale * scale) + linear
        z = q_ref[...].astype(F32) * (y * (0.5 * scale * scale) + linear)
        count = (length * (seq * n_ctx + ctx)).astype(F32)
        rden[...] = 1.0 / (den[...] + dot2r(indicator(), split(z), NT) + count)

    def query_state(scan, head):
        phi = features(qt[narrow(head), :])
        high, low = split(phi)
        phiq[head, 0:ROWS, :] = high
        phiq[head, ROWS : 2 * ROWS, :] = low
        phiq[head, 2 * ROWS : 3 * ROWS, :] = high
        scan.put(head, dot2(split(phi * rden[one(head), :]), g_ref[:, wide(head)]))
        scan.begin(head)

    def local_values(head):
        kern = kernel_of(scores(head)) * rden[one(head), :]
        gv_acc[head] = dot2(split(kern), g_ref[:, wide(head)])

    def middle(scan, head):
        g = g_ref[:, wide(head)]
        high, low = split(weighed(scan.result(head)))
        row = rden[one(head), :]
        state = jnp.concatenate([high, high, low], axis=0)
        out = (numer[head] + dot(state, phiq[head], TN)) * row
        out_ref[:, wide(head)] = out.T.astype(BF16)
        share = jnp.sum(g.astype(F32).T * out, axis=0, keepdims=True) * row
        shares[one(head), :] = share
        grad = dot(jnp.concatenate([high, low], axis=1), jnp.concatenate([g, g], axis=1), NT)
        gqt[narrow(head), :] = pull(grad, qt[narrow(head), :]) * row

    def local_gradients(head):
        s = scores(head)
        direct = dot(v_ref[:, wide(head)], g_ref[:, wide(head)], NT)
        direct = direct * rden[one(head), :] - shares[one(head), :]
        grad = split(jnp.where(causal(), direct * (1.0 + s), 0.0))
        gqt[narrow(head), :] += dot2r(kt16[narrow(head), :], grad) * scale
        gkt[narrow(head), :] = dot2r(qt16[narrow(head), :], grad, NT)

    def share_start(_):
        spread = dot2(split(shares[...]), indicator(), TN)
        gq_ref[...] = (gqt[...].T - spread * yn[...]).astype(BF16)
        part = split(q_ref[...].astype(F32) * spread)
        pulls.own[0:QK_DIM, :] = compact(dot2r(q_ref[...], part, TN))
        pulls.own[QK_DIM:, :] = dot2r(jnp.ones((8, length), BF16), part)
        pulls.start()

    def share_turn(_):
        pulls.turn()

    def last(scan, head):
        v = v_ref[:, wide(head)]
        high, low = split(weighed(scan.result(head)))
        state = jnp.concatenate([high, high, low], axis=0)
        grad_v = gv_acc[head] + dot(phik[head], state, TN)
        gv_ref[:, wide(head)] = grad_v.astype(BF16)
        grad = dot(jnp.concatenate([high, low], axis=1), jnp.concatenate([v, v], axis=1), NT)
        gkt[narrow(head), :] += pull(grad, kt[narrow(head), :])

    def values_too(scan, head):
        query_state(scan, head)
        local_values(head)

    def gradients_too(scan, head):
        middle(scan, head)
        local_gradients(head)

    plan, work, share_at, end = [], [], 0, 0
    for scan, start, lags in earlier:
        stages, done = scan.stages(start, lags)
        plan += stages
        work.append(scan.heads(functools.partial(gradients_too, scan), done))
        share_at = max(share_at, done + (scan.count - 1) * PIECES + 1)
    for scan, start, lags in later:
        stages, done = scan.stages(start, lags)
        plan = stages + plan
        work.append(scan.heads(functools.partial(values_too, scan), start))
        work.append(scan.heads(functools.partial(last, scan), done))
        end = max(end, done + (scan.count - 1) * PIECES + 1)
    end = max(end, share_at + SHARE_LAG + 1)
    plan += [(norm_turn, NORM_TURN, 1, 1, None), (norm_done, NORM_DONE, 1, 1, None)] + work
    plan += [(share_start, share_at, 1, 1, None), (share_turn, share_at + SHARE_LAG, 1, 1, None)]

    def turn(u, carry):
        for half in range(PIECES):
            for body, start, stride, count, condition in plan:
                if isinstance(start, int) and (stride == PIECES or count == 1):
                    if (half - start) % PIECES:
                        continue
                    item = u - (start - half) // PIECES
                else:
                    past = u * PIECES + half - start
                    item = past // stride
                if count == 1:
                    ok = item == 0
                else:
                    ok = (item >= 0) & (item < count)
                if stride > 1 and not isinstance(start, int):
                    ok = ok & (past % stride == 0)

                @pl.when(ok if condition is None else ok & condition)
                def _(body=body, item=item):
                    body(item)

        return carry

    lax.fori_loop(0, (end + PIECES - 1) // PIECES, turn, 0)
    after = pulls.result()
    square = split(blocks(after[:QK_DIM]))
    norm = dot2r(k_ref[...], square) * (scale * scale) + after[QK_DIM : QK_DIM + 1, :] * scale
    gk_ref[...] = (gkt[...].T - norm).astype(BF16)

    for scan, _, _ in earlier + later:
        scan.finish()
    norms.finish()
    pulls.finish()


def deliver(*refs):
    sem = refs[8]
    copies = [pltpu.make_async_copy(refs[i], refs[4 + i], sem.at[i]) for i in range(4)]
    for copy in copies:
        copy.start()
    for copy in copies:
        copy.wait()


def small_refs(n_ctx, n_seq):
    rows = QK_DIM + 8
    one = pltpu.VMEM((rows, LANES), F32)
    semaphores = pltpu.SemaphoreType.DMA((2,))
    return [
        one, pltpu.VMEM((n_ctx - 1, rows, LANES), F32), one, one,
        pltpu.VMEM((n_seq - 1, rows, LANES), F32), semaphores, semaphores,
    ]


def scan_refs(n_seq):
    rounds = radices(n_seq // 2)
    slots = sum(rounds) - len(rounds)
    full = pltpu.VMEM((HEADS, ROWS, LANES), F32)
    parts = pltpu.VMEM((len(rounds), HEADS, HALF, LANES), F32)
    halves = pltpu.VMEM((slots, HEADS, HALF, LANES), F32)
    send = pltpu.SemaphoreType.DMA((slots + 4,))
    chain = pltpu.SemaphoreType.DMA((2, CHUNKS))
    receive = pltpu.SemaphoreType.DMA((len(rounds) + 2, HEADS))
    return [full, full, full, parts, halves, full, full, full, full, full, send, chain, receive]


def per_device(n_ctx, n_seq, queries, keys, values, grad_output):
    length = queries.shape[0]
    across = pltpu.VMEM((LANES, length), F32)
    across16 = pltpu.VMEM((LANES, length), BF16)
    rows = pltpu.VMEM((HEADS, length), F32)
    stacked = pltpu.VMEM((HEADS, 3 * ROWS, length), BF16)
    narrow, broad = pltpu.VMEM(queries.shape, BF16), pltpu.VMEM(values.shape, BF16)
    scratch = [
        narrow, narrow, broad, broad, pltpu.SemaphoreType.DMA((4,)),
        across, across, across16, across16, rows, rows, rows,
        pltpu.VMEM((length, LANES), F32),
        pltpu.VMEM((HEADS, HEAD_DIM, length), F32),
        pltpu.VMEM((HEADS, length, HEAD_DIM), F32),
        across, across, stacked, stacked,
    ]
    scratch += small_refs(n_ctx, n_seq) * 2 + scan_refs(n_seq) * 2
    anywhere = pl.BlockSpec(memory_space=pl.ANY)
    inside = pl.BlockSpec(memory_space=pltpu.VMEM)
    results = pl.pallas_call(
        functools.partial(kernel, n_ctx, n_seq),
        out_shape=(broad, narrow, narrow, broad),
        in_specs=[anywhere] * 4,
        out_specs=(inside,) * 4,
        scratch_shapes=scratch,
        compiler_params=pltpu.CompilerParams(
            collective_id=0, has_side_effects=True, vmem_limit_bytes=56 << 20
        ),
        name="attention",
    )(queries, keys, values, grad_output)
    return pl.pallas_call(
        deliver,
        out_shape=tuple(jax.ShapeDtypeStruct(a.shape, a.dtype) for a in results),
        in_specs=[inside] * 4,
        out_specs=(anywhere,) * 4,
        scratch_shapes=[pltpu.SemaphoreType.DMA((4,))],
        name="deliver",
    )(*(pltpu.with_memory_space_constraint(a, pltpu.VMEM) for a in results))


def solution(mesh):
    placed = P(("seq", "ctx"), None)
    return jax.shard_map(
        functools.partial(per_device, mesh.shape["ctx"], mesh.shape["seq"]),
        mesh=mesh,
        in_specs=(placed,) * 4,
        out_specs=(placed,) * 4,
        check_vma=False,
    )
```
